32 devices in a mesh: box: 16 (over z, x, core), shift: 2 (over y).
Axes of the slice: x: 2, y: 2, z: 4, core: 2. Of those that a mesh axis runs over, the one named last changes fastest.
Arguments:
- vectors: bfloat16 [2, 1024, 128, 128], P('shift', 'box'), may hold values from -6 to 6
- sigma: float32 [2, 2], P('shift'), may hold values from 0.5 to 2
- near_blocks: bfloat16 [1024, 6, 128, 128], P('box', None, 'shift'), may hold values from -0.21875 to 0.21875
- near_index: int32 [1024, 6], P('box'), may hold values from -1 to 1023, as said below
- radiate: bfloat16 [128, 128], replicated, may hold values from -0.5 to 0.5
- interp_one: bfloat16 [8, 512, 128], replicated, may hold values from -0.1875 to 0.1875
- interp_two: bfloat16 [8, 2048, 512], replicated, may hold values from -0.09375 to 0.09375
- trans_one: float32 [316, 512], replicated, may hold values from -1.5 to 1.5
- level1_source: int32 [128, 16], P('box'), may hold values from -1 to 127, as said below
- level1_offset: int32 [128, 16], P('box'), may hold values from 0 to 315
- trans_two: float32 [316, 2048], P(None, 'box'), may hold values from -1 to 1
- level2_source: int32 [16, 32], replicated, may hold values from -1 to 15, as said below
- level2_offset: int32 [16, 32], replicated, may hold values from 0 to 315
Outputs:
- applied: float32 [2, 1024, 128, 128], P('shift', 'box')
The draws below stay inside these ranges and needn't reach their ends.
Inputs may be any that keep to these rules, and one draw needn't show every extreme that they name: `near_index`: leaf boxes are numbered along a space-filling curve. Entry 0 of each row is the box itself; every live entry names a box within 64 of the row's box; live entries come first, unused ones are -1; some rows use all 6 entries and some only one. `level1_source`: entry 0 of each row is live; every live entry names a box within 8 of the row's box; live entries come first, unused ones are -1; some rows use all 16 entries and some only one. `level2_source`: entry 0 of each row is live; live entries come first, unused ones are -1; some rows use all 32 entries and some only one.
All inputs are finite; a program needn't handle non-finite values.
Results may differ from the reference program's by a relative error of at most 0.0035.
Values may be sent and summed in bfloat16 or wider, within the bound.
No kernel may reach another device: no remote copies, remote signals or barrier semaphores. Data moves between devices by JAX's collectives and lax.ppermute only.
A program may use at most 192 MiB of HBM per device.

```python
import jax
import jax.numpy as jnp
from jax import lax

U = 128
K0R = 128
K1R = 512
K2R = 2048
R = 128
BOX_DEV = 64
NN = 6
M1 = 16
M2 = 32
NOFF = 316
SHIFTS = 2
NB = 1024
NB1 = 128
NB2 = 16


def ragged_lists(key, rows_total, width, reach):
    key_count = jax.random.fold_in(key, 11)
    key_step = jax.random.fold_in(key, 12)
    rows = jnp.arange(rows_total)
    count = jax.random.randint(key_count, (rows_total,), 1, width + 1)
    count = jnp.where(rows % 16 == 0, width, count)
    count = jnp.where(rows % 16 == 8, 1, count)
    step = jax.random.randint(key_step, (rows_total, width), -reach, reach + 1)
    step = step.at[:, 0].set(jnp.abs(step[:, 0]))
    ids = jnp.clip(rows[:, None] + step, 0, rows_total - 1)
    slots = jnp.arange(width)[None, :]
    return (ids, slots < count[:, None])


def draw_near_index(key, part):
    ids, live = ragged_lists(key, NB, NN, BOX_DEV)
    ids = ids.at[:, 0].set(jnp.arange(NB))
    return jnp.where(live, ids, -1).astype(jnp.int32)


def draw_level1_source(key, part):
    ids, live = ragged_lists(key, NB1, M1, BOX_DEV // 8)
    return jnp.where(live, ids, -1).astype(jnp.int32)


def draw_level2_source(key, part):
    ids, live = ragged_lists(key, NB2, M2, 1)
    far_ids = jax.random.randint(jax.random.fold_in(key, 13), (NB2, M2), 0, NB2)
    rows = jnp.arange(NB2)
    far_ids = far_ids.at[:, 0].set((rows + NB2 // 2) % NB2)
    return jnp.where(live, far_ids, -1).astype(jnp.int32)


def touch_ends(entries, key, least, high):
    index_at = [jax.random.randint(jax.random.fold_in(key, axis), (), 0, length) for axis, length in enumerate(entries.shape)]
    longest = entries.shape.index(max(entries.shape))
    beside = index_at[:longest] + [(index_at[longest] + 1) % entries.shape[longest]] + index_at[longest + 1:]
    return entries.at[tuple(index_at)].set(least).at[tuple(beside)].set(high)


def level_of(key, shape, shards, least, high):
    def one(dim, parts):
        heights = jax.random.uniform(jax.random.fold_in(jax.random.fold_in(key, 6), dim), (parts,), jnp.float32, least / len(shards), high / len(shards))
        return jnp.repeat(jnp.exp(heights), shape[dim] // parts).reshape((-1,) + (1,) * (len(shape) - dim - 1))

    factor_of = one(*shards[0])
    for cut in shards[1:]:
        factor_of = factor_of * one(*cut)
    return factor_of


def centred(key, shape, scale, limit, cuts=(), kind=jnp.bfloat16):
    gain = level_of(key, shape, cuts, -0.22, 0.18) if cuts else 1.0
    result = jax.random.normal(key, shape, jnp.float32) * scale * gain
    return jnp.minimum(jnp.maximum(result, -limit), limit).astype(kind)


def setup_inputs(seed: int = 0) -> dict:
    key_of = jax.random.split(jax.random.key(seed), 14)
    vectors = centred(key_of[0], (SHIFTS, NB, U, R), 1.0, 6.0, ((0, 2), (1, 16)))
    sigma = jnp.clip(0.5 + 1.5 * jax.random.uniform(key_of[1], (SHIFTS, 2), jnp.float32) ** level_of(key_of[1], (SHIFTS, 2), ((0, 2),), -0.2, 0.2), 0.5, 2.0)
    near_blocks = centred(key_of[2], (NB, NN, U, U), (U * NN) ** -0.5, 0.21875, ((0, 16), (2, 2)))
    near_index = draw_near_index(jax.random.fold_in(key_of[13], 71), 0)
    radiate = centred(key_of[4], (K0R, U), U ** -0.5, 0.5)
    interp_one = centred(key_of[5], (8, K1R, K0R), (8 * K0R) ** -0.5, 0.1875)
    interp_two = centred(key_of[6], (8, K2R, K1R), (8 * K1R) ** -0.5, 0.09375)
    trans_one = centred(key_of[7], (NOFF, K1R), M1 ** -0.5, 1.5, (), jnp.float32)
    level1_source = draw_level1_source(jax.random.fold_in(key_of[13], 71), 0)
    level1_offset = touch_ends(jax.random.randint(key_of[9], (NB1, M1), 0, NOFF), jax.random.fold_in(key_of[9], 1), 0, NOFF - 1).astype(jnp.int32)
    trans_two = centred(key_of[10], (NOFF, K2R), M2 ** -0.5, 1.0, ((1, 16),), jnp.float32)
    level2_source = draw_level2_source(jax.random.fold_in(key_of[13], 71), 0)
    level2_offset = touch_ends(jax.random.randint(key_of[12], (NB2, M2), 0, NOFF), jax.random.fold_in(key_of[12], 1), 0, NOFF - 1).astype(jnp.int32)
    return dict(vectors=vectors, sigma=sigma, near_blocks=near_blocks, near_index=near_index, radiate=radiate, interp_one=interp_one, interp_two=interp_two, trans_one=trans_one, level1_source=level1_source, level1_offset=level1_offset, trans_two=trans_two, level2_source=level2_source, level2_offset=level2_offset)


def near_product(field, near_blocks, near_index):
    groups = NB // BOX_DEV
    blocks = near_blocks.reshape(groups, BOX_DEV, NN, U, U)
    ids = near_index.reshape(groups, BOX_DEV, NN)

    def one_group(pair):
        block_part, id_part = pair
        live = id_part >= 0
        safe = jnp.where(live, id_part, 0).astype(jnp.int32)
        source = field[safe] * live[:, :, None, None].astype(field.dtype)
        return jnp.einsum('bjvu,bjur->bvr', block_part.astype(jnp.float32), source.astype(jnp.float32))

    return lax.map(one_group, (blocks, ids)).reshape(NB, U, R)


def translate(pattern, table, offsets, sources):
    def one_box(pair):
        off_row, src_row = pair
        live = src_row >= 0
        safe = jnp.where(live, src_row, 0).astype(jnp.int32)
        weights = table[off_row] * live[:, None].astype(jnp.float32)
        return jnp.einsum('jk,jkr->kr', weights, pattern[safe].astype(jnp.float32))

    return lax.map(one_box, (offsets, sources))


def reference(vectors, sigma, near_blocks, near_index, radiate, interp_one, interp_two, trans_one, level1_source, level1_offset, trans_two, level2_source, level2_offset):
    results = []
    for shift_id in range(SHIFTS):
        field = vectors[shift_id]
        near = near_product(field, near_blocks, near_index)
        leaf = jnp.einsum('ku,bur->bkr', radiate.astype(jnp.float32), field.astype(jnp.float32)).astype(jnp.bfloat16)
        upper = jnp.einsum('oqk,cokr->cqr', interp_one.astype(jnp.float32), leaf.reshape(NB1, 8, K0R, R).astype(jnp.float32)).astype(jnp.bfloat16)
        coarse = jnp.einsum('oqk,gokr->gqr', interp_two.astype(jnp.float32), upper.reshape(NB2, 8, K1R, R).astype(jnp.float32)).astype(jnp.bfloat16)
        incoming = translate(coarse, trans_two, level2_offset, level2_source).astype(jnp.bfloat16)
        across = translate(upper, trans_one, level1_offset, level1_source)
        down = jnp.einsum('oqk,gqr->gokr', interp_two.astype(jnp.float32), incoming.astype(jnp.float32)).reshape(NB1, K1R, R)
        local_in = (across + down).astype(jnp.bfloat16)
        leaf_in = jnp.einsum('oqk,cqr->cokr', interp_one.astype(jnp.float32), local_in.astype(jnp.float32)).reshape(NB, K0R, R).astype(jnp.bfloat16)
        far = jnp.einsum('ku,bkr->bur', radiate.astype(jnp.float32), leaf_in.astype(jnp.float32))
        real_part = field[:, : U // 2].astype(jnp.float32)
        imag_part = field[:, U // 2:].astype(jnp.float32)
        sig_re = sigma[shift_id, 0]
        sig_im = sigma[shift_id, 1]
        scaled = jnp.concatenate([sig_re * real_part - sig_im * imag_part, sig_re * imag_part + sig_im * real_part], axis=1)
        results.append(near + far - scaled)
    return jnp.stack(results)
```

```python
import functools

import jax
import jax.numpy as jnp
from jax import lax
from jax.experimental import pallas as pl
from jax.experimental.pallas import tpu as pltpu
from jax.sharding import PartitionSpec as P


F32 = jnp.float32
BF16 = jnp.bfloat16
VMEM_LIMIT = 56 << 20
NT = (((1,), (1,)), ((), ()))


def vmem():
    return pl.BlockSpec(memory_space=pltpu.VMEM)


def smem():
    return pl.BlockSpec(memory_space=pltpu.SMEM)


def cost(flops, moved):
    return pl.CostEstimate(flops=flops, bytes_accessed=moved, transcendentals=0)


def params(**more):
    return pltpu.CompilerParams(vmem_limit_bytes=VMEM_LIMIT, **more)


def fold_kernel(one_ref, radiate_ref, field_ref, fold_ref, upper_ref, turned_ref):
    children, samples1, _ = one_ref.shape
    unknowns = radiate_ref.shape[1]
    for child in range(children):
        fold_ref[:, child * unknowns : (child + 1) * unknowns] = jnp.dot(
            one_ref[child], radiate_ref[...], preferred_element_type=F32
        ).astype(BF16)

    def step(parent, carry):
        pattern = jnp.dot(fold_ref[...], field_ref[parent], preferred_element_type=F32)
        upper_ref[parent] = pattern.astype(BF16)
        turned_ref[parent] = pattern.T.astype(BF16)
        return carry

    lax.fori_loop(0, field_ref.shape[0], step, 0)


def fold(interp_one, radiate, field):
    children, samples1, samples0 = interp_one.shape
    unknowns = radiate.shape[1]
    parents, _, columns = field.shape
    return pl.pallas_call(
        fold_kernel,
        out_shape=(
            jax.ShapeDtypeStruct((samples1, children * unknowns), BF16),
            jax.ShapeDtypeStruct((parents, samples1, columns), BF16),
            jax.ShapeDtypeStruct((parents, columns, samples1), BF16),
        ),
        in_specs=[vmem()] * 3,
        out_specs=(vmem(),) * 3,
        compiler_params=params(),
        cost_estimate=cost(3 * 10**9, 6 * 2**20),
        name="fold",
    )(interp_one, radiate, field)


def coarse_kernel(two_ref, upper_ref, out_ref):
    total = jnp.dot(two_ref[0], upper_ref[0], preferred_element_type=F32)
    for child in range(1, two_ref.shape[0]):
        total += jnp.dot(two_ref[child], upper_ref[child], preferred_element_type=F32)
    out_ref[0] = total.astype(BF16)


def coarsen(interp_two, upper):
    children, samples2, samples1 = interp_two.shape
    parents, _, columns = upper.shape
    grand = parents // children
    rows = min(samples2, 256)
    return pl.pallas_call(
        coarse_kernel,
        grid=(samples2 // rows, grand),
        out_shape=jax.ShapeDtypeStruct((grand, samples2, columns), BF16),
        in_specs=[
            pl.BlockSpec((children, rows, samples1), lambda q, g: (0, q, 0)),
            pl.BlockSpec((children, samples1, columns), lambda q, g: (g, 0, 0)),
        ],
        out_specs=pl.BlockSpec((1, rows, columns), lambda q, g: (g, q, 0)),
        compiler_params=params(),
        cost_estimate=cost(4 * 10**9, 18 * 2**20),
        name="coarsen",
    )(interp_two, upper)


def live_count(source_ref, row):
    total = jnp.int32(0)
    for slot in range(source_ref.shape[1]):
        total += (source_ref[row, slot] >= 0).astype(jnp.int32)
    return total


def level2_kernel(offset_ref, source_ref, table_ref, pattern_ref, out_ref, turned_ref):
    boxes = pattern_ref.shape[0]

    def turn(box, carry):
        turned_ref[box] = pattern_ref[box].astype(F32).T
        return carry

    lax.fori_loop(0, boxes, turn, 0)

    def per_box(box, carry):
        def add(slot, total):
            weight = table_ref[pl.ds(offset_ref[box, slot], 1), :]
            return total + weight * turned_ref[source_ref[box, slot]]

        total = lax.fori_loop(
            0, live_count(source_ref, box), add, jnp.zeros(turned_ref.shape[1:], F32)
        )
        out_ref[box] = total.astype(BF16)
        return carry

    lax.fori_loop(0, out_ref.shape[0], per_box, 0)


def level2(offset, source, table, pattern):
    boxes, samples, columns = pattern.shape
    return pl.pallas_call(
        level2_kernel,
        out_shape=jax.ShapeDtypeStruct((offset.shape[0], columns, samples), BF16),
        in_specs=[smem(), smem(), vmem(), vmem()],
        out_specs=vmem(),
        scratch_shapes=[pltpu.VMEM((boxes, columns, samples), F32)],
        compiler_params=params(),
        cost_estimate=cost(3 * 10**9, 2 * 2**20),
        name="level2",
    )(offset, source, table, pattern)


def weighted_lists(pattern, table, offsets, sources):
    live = sources >= 0
    weights = table[offsets] * live[:, :, None].astype(F32)
    picked = pattern[jnp.where(live, sources, 0)]
    return jnp.einsum("cjk,cjkr->ckr", weights, picked, preferred_element_type=F32)


def level1_kernel(
    place_ref, offset_ref, source_ref, table_ref, fold_ref, low_ref, high_ref, own_ref,
    out_ref, unfold_ref, rim_ref, rows_ref,
):
    parents, columns, samples1 = own_ref.shape
    width = rows_ref.shape[2]
    for part in range(rows_ref.shape[0]):
        rows_ref[part] = table_ref[:, part * width : (part + 1) * width]

    def rise(parent, carry):
        low = jnp.dot(fold_ref[...], low_ref[parent], preferred_element_type=F32)
        rim_ref[parent] = low.T.astype(BF16).astype(F32)
        rim_ref[parents + parent] = own_ref[parent].astype(F32)
        high = jnp.dot(fold_ref[...], high_ref[parent], preferred_element_type=F32)
        rim_ref[2 * parents + parent] = high.T.astype(BF16).astype(F32)
        return carry

    lax.fori_loop(0, parents, rise, 0)
    step = 128
    for first in range(0, fold_ref.shape[1], step):
        unfold_ref[first : first + step, :] = fold_ref[:, first : first + step].T
    base = place_ref[0] * parents - parents

    def per_box(box, carry):
        count = live_count(source_ref, box)
        for part in range(samples1 // width):
            first = part * width

            def add(slot, total):
                weight = rows_ref[part, pl.ds(offset_ref[box, slot], 1), :]
                return total + weight * rim_ref[source_ref[box, slot] - base, :, first : first + width]

            out_ref[box, :, first : first + width] = lax.fori_loop(
                0, count, add, jnp.zeros((columns, width), F32)
            )
        return carry

    lax.fori_loop(0, parents, per_box, 0)


def level1(place, offset, source, table, folded, low, high, own):
    parents, columns, samples1 = own.shape
    return pl.pallas_call(
        level1_kernel,
        out_shape=(
            jax.ShapeDtypeStruct((parents, columns, samples1), F32),
            jax.ShapeDtypeStruct((folded.shape[1], folded.shape[0]), BF16),
        ),
        in_specs=[smem()] * 3 + [vmem()] * 5,
        out_specs=(vmem(), vmem()),
        scratch_shapes=[
            pltpu.VMEM((3 * parents, columns, samples1), F32),
            pltpu.VMEM((samples1 // 128, table.shape[0], 128), F32),
        ],
        compiler_params=params(),
        cost_estimate=cost(8 * 10**9, 10 * 2**20),
        name="level1",
    )(place, offset, source, table, folded, low, high, own)


def near_kernel(
    place_ref, index_ref, blocks_ref, low_ref, own_ref, high_even_ref, high_odd_ref,
    out_ref, field_ref, sem, *, first,
):
    step = pl.program_id(0)
    boxes = own_ref.shape[0]
    chunk, slots, rows, unknowns = blocks_ref.shape
    place = place_ref[0]

    def copies():
        return (
            pltpu.make_async_copy(low_ref, field_ref.at[pl.ds(0, boxes)], sem.at[0]),
            pltpu.make_async_copy(own_ref, field_ref.at[pl.ds(boxes, boxes)], sem.at[1]),
        )

    def high(ref):
        return pltpu.make_async_copy(ref, field_ref.at[pl.ds(2 * boxes, boxes)], sem.at[2])

    @pl.when(step == 0)
    def _():
        for copy in copies():
            copy.start()
        if high_even_ref is high_odd_ref:
            high(high_even_ref).start()
        else:

            @pl.when(place % 2 == 0)
            def _():
                high(high_even_ref).start()

            @pl.when(place % 2 == 1)
            def _():
                high(high_odd_ref).start()

        for copy in copies():
            copy.wait()
        high(high_even_ref).wait()

    base = place * boxes - boxes
    for box in range(chunk):
        row = first + step * chunk + box
        total = None
        for slot in range(0, slots, 2):
            left, right = [], []
            for one in range(slot, min(slot + 2, slots)):
                block = blocks_ref[box, one]
                if one == 0:
                    where = boxes + row
                else:
                    named = index_ref[row, one]
                    live = named >= 0
                    where = jnp.where(live, named - base, boxes)
                    block = jnp.where(live, block, jnp.zeros_like(block))
                left.append(block)
                right.append(field_ref[where])
            part = jnp.dot(
                jnp.concatenate(left, axis=1),
                jnp.concatenate(right, axis=0),
                preferred_element_type=F32,
            )
            total = part if total is None else total + part
        out_ref[box] = total.astype(out_ref.dtype)


def near(place, index, blocks, low, own, high_even, high_odd, first, count, kind, name):
    boxes, unknowns, columns = own.shape
    _, slots, rows, _ = blocks.shape
    chunk = min(8, count)
    if high_even is high_odd:

        def kernel(place_ref, index_ref, blocks_ref, low_ref, own_ref, high_ref, *rest):
            near_kernel(
                place_ref, index_ref, blocks_ref, low_ref, own_ref, high_ref, high_ref, *rest,
                first=first,
            )

        highs = (high_even,)
    else:
        kernel = functools.partial(near_kernel, first=first)
        highs = (high_even, high_odd)
    hbm = pl.BlockSpec(memory_space=pl.ANY)
    return pl.pallas_call(
        kernel,
        grid=(count // chunk,),
        out_shape=jax.ShapeDtypeStruct((count, rows, columns), kind),
        in_specs=[
            smem(),
            smem(),
            pl.BlockSpec((chunk, slots, rows, unknowns), lambda i: (first // chunk + i, 0, 0, 0)),
        ]
        + [hbm] * (2 + len(highs)),
        out_specs=pl.BlockSpec((chunk, rows, columns), lambda i: (i, 0, 0)),
        scratch_shapes=[
            pltpu.VMEM((3 * boxes, unknowns, columns), BF16),
            pltpu.SemaphoreType.DMA((3,)),
        ],
        compiler_params=params(),
        cost_estimate=cost(count * 10**8, 8 * 2**20 + count * 10**5),
        name=name,
    )(place, index, blocks, low, own, *highs)


def down_kernel(
    place_ref, sigma_ref, inc_ref, two_ref, across_ref, unfold_ref, field_ref, near_ref,
    out_ref, flat_ref, *, children, shifts,
):
    chunks, _, lanes = inc_ref.shape[1:]

    @pl.when(pl.program_id(0) % children == 0)
    def _():
        for one in range(chunks):
            flat_ref[:, one * lanes : (one + 1) * lanes] = inc_ref[0, one]

    down = jnp.dot(flat_ref[...], two_ref[0], preferred_element_type=F32)
    local = (down + across_ref[0]).astype(BF16)
    far = lax.dot_general(unfold_ref[...], local, NT, preferred_element_type=F32)
    boxes, unknowns, columns = out_ref.shape
    far = far.reshape(boxes, unknowns, columns)
    half = unknowns // 2
    real = field_ref[:, :half, :].astype(F32)
    imag = field_ref[:, half:, :].astype(F32)
    re, im = sigma_ref[0, 0], sigma_ref[0, 1]
    out_ref[:, :half, :] = far[:, :half] - (re * real - im * imag)
    out_ref[:, half:, :] = far[:, half:] - (re * imag + im * real)
    rows = near_ref.shape[1]
    for shift in range(shifts):

        @pl.when(place_ref[1] == shift)
        def _():
            out_ref[:, shift * rows : (shift + 1) * rows, :] += near_ref[...]


def downward(place, sigma, inc, interp_two, across, unfold, field, near_own, shifts):
    grand, chunks, columns, lanes = inc.shape
    children, samples2, samples1 = interp_two.shape
    boxes, unknowns, _ = field.shape
    rows = near_own.shape[1]
    per = boxes // across.shape[0]
    return pl.pallas_call(
        functools.partial(down_kernel, children=children, shifts=shifts),
        grid=(grand * children,),
        out_shape=jax.ShapeDtypeStruct((boxes, unknowns, columns), F32),
        in_specs=[
            smem(),
            smem(),
            pl.BlockSpec((1, chunks, columns, lanes), lambda c: (c // children, 0, 0, 0)),
            pl.BlockSpec((1, samples2, samples1), lambda c: (c % children, 0, 0)),
            pl.BlockSpec((1, columns, samples1), lambda c: (c, 0, 0)),
            pl.BlockSpec(unfold.shape, lambda c: (0, 0)),
            pl.BlockSpec((per, unknowns, columns), lambda c: (c, 0, 0)),
            pl.BlockSpec((per, rows, columns), lambda c: (c, 0, 0)),
        ],
        out_specs=pl.BlockSpec((per, unknowns, columns), lambda c: (c, 0, 0)),
        scratch_shapes=[pltpu.VMEM((columns, chunks * lanes), BF16)],
        compiler_params=params(),
        cost_estimate=cost(6 * 10**9, 30 * 2**20),
        name="downward",
    )(place, sigma, inc, interp_two, across, unfold, field, near_own)


def join_kernel(place_ref, total_ref, part_ref, out_ref):
    out_ref[...] = total_ref[...] + part_ref[...].astype(F32)


def join(place, total, part, first, name):
    boxes, unknowns, columns = total.shape
    count, rows, _ = part.shape
    step = min(16, count)
    half = pl.BlockSpec((step, rows, columns), lambda i, place_ref: (first // step + i, 1 - place_ref[1], 0))
    return pl.pallas_call(
        join_kernel,
        grid_spec=pltpu.PrefetchScalarGridSpec(
            num_scalar_prefetch=1,
            grid=(count // step,),
            in_specs=[half, pl.BlockSpec((step, rows, columns), lambda i, place_ref: (i, 0, 0))],
            out_specs=half,
        ),
        out_shape=jax.ShapeDtypeStruct(total.shape, F32),
        input_output_aliases={1: 0},
        compiler_params=params(),
        cost_estimate=cost(10**7, 2 * 2**20),
        name=name,
    )(place, total, part)


def body(
    vectors, sigma, near_blocks, near_index, radiate, interp_one, interp_two, trans_one,
    level1_source, level1_offset, trans_two, level2_source, level2_offset,
):
    field = vectors[0]
    boxes, unknowns, columns = field.shape
    children, samples1, _ = interp_one.shape
    samples2 = interp_two.shape[1]
    parents = boxes // children
    grand = parents // children
    count = lax.axis_size("box")
    shifts = lax.axis_size("shift")
    place = jnp.stack([lax.axis_index("box"), lax.axis_index("shift")]).astype(jnp.int32)

    up = [(i, i + 1) for i in range(count - 1)]
    down = [(i + 1, i) for i in range(count - 1)]
    swap = [(s, shifts - 1 - s) for s in range(shifts)]
    pair_down = [(i + 1, i) for i in range(0, count - 1, 2)]
    odd_swap = [
        (i * shifts + s, i * shifts + shifts - 1 - s) for i in range(1, count, 2) for s in range(shifts)
    ]

    other = lax.ppermute(field, "shift", swap)
    high = lax.ppermute(field, "box", down)
    low = lax.ppermute(field, "box", up)

    folded, upper, turned = fold(
        interp_one, radiate, field.reshape(parents, children * unknowns, columns)
    )
    coarse = coarsen(interp_two, upper)
    chunk = samples2 // count
    pieces = coarse.reshape(grand, count, chunk, columns).swapaxes(0, 1)
    spread = lax.all_to_all(pieces, "box", split_axis=0, concat_axis=0, tiled=True)
    spread = spread.reshape(count * grand, chunk, columns)
    if chunk % 128 == 0:
        inc = level2(level2_offset, level2_source, trans_two, spread)
        inc = lax.all_to_all(
            inc.reshape(count, grand, columns, chunk), "box", split_axis=0, concat_axis=0, tiled=True
        ).swapaxes(0, 1)
    else:
        inc = weighted_lists(spread, trans_two, level2_offset, level2_source).astype(BF16)
        inc = lax.all_to_all(
            inc.reshape(count, grand, chunk, columns), "box", split_axis=0, concat_axis=0, tiled=True
        ).swapaxes(0, 1)
        inc = inc.reshape(grand, samples2 // 128, 128, columns).swapaxes(2, 3)

    high_odd = lax.ppermute(high, ("box", "shift"), odd_swap)
    low_other = lax.ppermute(other, "box", up)
    high_even = lax.ppermute(other, "box", pair_down)

    wide = (parents, children * unknowns, columns)
    across, unfold = level1(
        place, level1_offset, level1_source, trans_one, folded,
        low.reshape(wide), high.reshape(wide), turned,
    )
    near_own = near(
        place, near_index, near_blocks, low, field, high, high, 0, boxes, F32, "near_own"
    )
    splits = 2
    part = boxes // splits
    arrived = []
    for one in range(splits):
        mine = near(
            place, near_index, near_blocks, low_other, other, high_even, high_odd,
            one * part, part, BF16, "near_other" + str(one),
        )
        arrived.append(lax.ppermute(mine, "shift", swap))

    total = downward(place, sigma, inc, interp_two, across, unfold, field, near_own, shifts)
    for one in range(splits):
        total = join(place, total, arrived[one], one * part, "join" + str(one))
    return total[None]


def solution(mesh):
    in_specs = (
        P("shift", "box", None, None),
        P("shift", None),
        P("box", None, "shift", None),
        P("box", None),
        P(),
        P(),
        P(),
        P(),
        P("box", None),
        P("box", None),
        P(None, "box"),
        P(),
        P(),
    )
    out_specs = P("shift", "box", None, None)
    return jax.shard_map(body, mesh=mesh, in_specs=in_specs, out_specs=out_specs, check_vma=False)
```

```python
import functools

import jax
import jax.numpy as jnp
from jax import lax
from jax.experimental import pallas as pl
from jax.experimental.pallas import tpu as pltpu
from jax.sharding import PartitionSpec as P


F32 = jnp.float32
BF16 = jnp.bfloat16
NT = (((1,), (1,)), ((), ()))


def vmem():
    return pl.BlockSpec(memory_space=pltpu.VMEM)


def smem():
    return pl.BlockSpec(memory_space=pltpu.SMEM)


def cost(flops, moved):
    return pl.CostEstimate(flops=flops, bytes_accessed=moved, transcendentals=0)


def params(mib):
    return pltpu.CompilerParams(vmem_limit_bytes=mib << 20)


def fold_kernel(one_ref, radiate_ref, field_ref, fold_ref, upper_ref, turned_ref):
    children, samples1, _ = one_ref.shape
    unknowns = radiate_ref.shape[1]
    pair, _, columns = field_ref.shape

    @pl.when(pl.program_id(0) == 0)
    def _():
        for child in range(children):
            fold_ref[:, child * unknowns : (child + 1) * unknowns] = jnp.dot(
                one_ref[child], radiate_ref[...], preferred_element_type=F32
            ).astype(BF16)

    wide = jnp.concatenate([field_ref[one] for one in range(pair)], axis=1)
    pattern = jnp.dot(fold_ref[...], wide, preferred_element_type=F32)
    for one in range(pair):
        mine = pattern[:, one * columns : (one + 1) * columns]
        upper_ref[one] = mine.astype(BF16)
        turned_ref[one] = mine.T.astype(BF16)


def fold(interp_one, radiate, field):
    children, samples1, samples0 = interp_one.shape
    unknowns = radiate.shape[1]
    parents, width, columns = field.shape
    pair = 2 if parents % 2 == 0 else 1
    return pl.pallas_call(
        fold_kernel,
        grid=(parents // pair,),
        out_shape=(
            jax.ShapeDtypeStruct((samples1, children * unknowns), BF16),
            jax.ShapeDtypeStruct((parents, samples1, columns), BF16),
            jax.ShapeDtypeStruct((parents, columns, samples1), BF16),
        ),
        in_specs=[
            pl.BlockSpec(interp_one.shape, lambda i: (0, 0, 0)),
            pl.BlockSpec(radiate.shape, lambda i: (0, 0)),
            pl.BlockSpec((pair, width, columns), lambda i: (i, 0, 0)),
        ],
        out_specs=(
            pl.BlockSpec((samples1, children * unknowns), lambda i: (0, 0)),
            pl.BlockSpec((pair, samples1, columns), lambda i: (i, 0, 0)),
            pl.BlockSpec((pair, columns, samples1), lambda i: (i, 0, 0)),
        ),
        compiler_params=params(56),
        cost_estimate=cost(3 * 10**9, 6 * 2**20),
        name="fold",
    )(interp_one, radiate, field)


def coarse_kernel(two_ref, upper_ref, out_ref):
    total = jnp.dot(two_ref[0], upper_ref[0], preferred_element_type=F32)
    for child in range(1, two_ref.shape[0]):
        total += jnp.dot(two_ref[child], upper_ref[child], preferred_element_type=F32)
    out_ref[0] = total.astype(BF16)


def coarsen(interp_two, upper):
    children, samples2, samples1 = interp_two.shape
    parents, _, columns = upper.shape
    grand = parents // children
    rows = min(samples2, 256)
    return pl.pallas_call(
        coarse_kernel,
        grid=(samples2 // rows, grand),
        out_shape=jax.ShapeDtypeStruct((grand, samples2, columns), BF16),
        in_specs=[
            pl.BlockSpec((children, rows, samples1), lambda q, g: (0, q, 0)),
            pl.BlockSpec((children, samples1, columns), lambda q, g: (g, 0, 0)),
        ],
        out_specs=pl.BlockSpec((1, rows, columns), lambda q, g: (g, q, 0)),
        compiler_params=params(56),
        cost_estimate=cost(4 * 10**9, 18 * 2**20),
        name="coarsen",
    )(interp_two, upper)


def live_count(source_ref, row):
    total = jnp.int32(0)
    for slot in range(source_ref.shape[1]):
        total += (source_ref[row, slot] >= 0).astype(jnp.int32)
    return total


def list_sum(offset_ref, source_ref, box, shape, weight_at, pattern_at, base):
    unroll = next(n for n in (4, 2, 1) if source_ref.shape[1] % n == 0)

    def add(trip, total):
        for one in range(unroll):
            slot = trip * unroll + one
            named = source_ref[box, slot]
            live = named >= 0
            weight = weight_at(offset_ref[box, slot]) * live.astype(F32)
            total = total + weight * pattern_at(jnp.where(live, named - base, 0))
        return total

    trips = (live_count(source_ref, box) + unroll - 1) // unroll
    return lax.fori_loop(0, trips, add, jnp.zeros(shape, F32))


def level2_kernel(offset_ref, source_ref, table_ref, pattern_ref, out_ref, turned_ref):
    boxes = pattern_ref.shape[0]

    def turn(box, carry):
        turned_ref[box] = pattern_ref[box].astype(F32).T
        return carry

    lax.fori_loop(0, boxes, turn, 0)

    def per_box(box, carry):
        total = list_sum(
            offset_ref, source_ref, box, turned_ref.shape[1:],
            lambda offset: table_ref[pl.ds(offset, 1), :], lambda source: turned_ref[source], 0,
        )
        out_ref[box] = total.astype(BF16)
        return carry

    lax.fori_loop(0, out_ref.shape[0], per_box, 0)


def level2(offset, source, table, pattern):
    boxes, samples, columns = pattern.shape
    return pl.pallas_call(
        level2_kernel,
        out_shape=jax.ShapeDtypeStruct((offset.shape[0], columns, samples), BF16),
        in_specs=[smem(), smem(), vmem(), vmem()],
        out_specs=vmem(),
        scratch_shapes=[pltpu.VMEM((boxes, columns, samples), F32)],
        compiler_params=params(8),
        cost_estimate=cost(3 * 10**9, 2 * 2**20),
        name="level2",
    )(offset, source, table, pattern)


def weighted_lists(pattern, table, offsets, sources):
    live = sources >= 0
    weights = table[offsets] * live[:, :, None].astype(F32)
    picked = pattern[jnp.where(live, sources, 0)]
    return jnp.einsum("cjk,cjkr->ckr", weights, picked, preferred_element_type=F32)


def field_copies(place, low_ref, own_ref, high_refs, field_ref, sem):
    boxes = own_ref.shape[0]

    def into(ref, which):
        return pltpu.make_async_copy(ref, field_ref.at[pl.ds(which * boxes, boxes)], sem.at[which])

    def start():
        into(low_ref, 0).start()
        into(own_ref, 1).start()
        for which, ref in enumerate(high_refs):

            @pl.when(place % len(high_refs) == which)
            def _():
                into(ref, 2).start()

    def wait():
        into(low_ref, 0).wait()
        into(own_ref, 1).wait()
        into(high_refs[0], 2).wait()

    return start, wait


def near_rows(place, index_ref, blocks_ref, field_ref, out_ref, row):
    boxes = field_ref.shape[0] // 3
    chunk, slots = blocks_ref.shape[:2]
    base = place * boxes - boxes
    for box in range(chunk):
        total = None
        for slot in range(0, slots, 2):
            left, right = [], []
            for one in range(slot, min(slot + 2, slots)):
                block = blocks_ref[box, one]
                if one == 0:
                    where = boxes + row + box
                else:
                    named = index_ref[one, row + box]
                    live = named >= 0
                    where = jnp.where(live, named - base, boxes)
                    block = jnp.where(live, block, jnp.zeros_like(block))
                left.append(block)
                right.append(field_ref[where])
            part = jnp.dot(
                jnp.concatenate(left, axis=1),
                jnp.concatenate(right, axis=0),
                preferred_element_type=F32,
            )
            total = part if total is None else total + part
        out_ref[box] = total.astype(out_ref.dtype)


def own_kernel(
    place_ref, index_ref, offset_ref, source_ref, table_ref, fold_ref, turned_ref, blocks_ref,
    low_ref, own_ref, high_ref, near_ref, across_ref, unfold_ref,
    field_ref, rim_ref, rows_ref, sem,
):
    step = pl.program_id(0)
    parents, columns, samples1 = turned_ref.shape
    children = blocks_ref.shape[0]
    boxes = own_ref.shape[0]
    unknowns = field_ref.shape[1]
    width = rows_ref.shape[2]
    place = place_ref[0]
    start, wait = field_copies(place, low_ref, own_ref, (high_ref,), field_ref, sem)

    @pl.when(step == 0)
    def _():
        start()
        for part in range(rows_ref.shape[0]):
            rows_ref[part] = table_ref[:, part * width : (part + 1) * width]
        for first in range(0, fold_ref.shape[1], 128):
            unfold_ref[first : first + 128, :] = fold_ref[:, first : first + 128].T
        for parent in range(parents):
            rim_ref[parents + parent] = turned_ref[parent].astype(F32)
        wait()

    near_rows(place, index_ref, blocks_ref, field_ref, near_ref, step * children)
    low = field_ref[pl.ds(step * children, children)].reshape(children * unknowns, columns)
    high = field_ref[pl.ds(2 * boxes + step * children, children)].reshape(children * unknowns, columns)
    both = jnp.dot(
        fold_ref[...], jnp.concatenate([low, high], axis=1), preferred_element_type=F32
    )
    rim_ref[step] = both[:, :columns].T.astype(BF16).astype(F32)
    rim_ref[2 * parents + step] = both[:, columns:].T.astype(BF16).astype(F32)

    @pl.when(step == parents - 1)
    def _():
        def per_box(box, carry):
            for part in range(samples1 // width):
                lanes = slice(part * width, (part + 1) * width)
                across_ref[box, :, lanes] = list_sum(
                    offset_ref, source_ref, box, (columns, width),
                    lambda offset: rows_ref[part, pl.ds(offset, 1), :],
                    lambda source: rim_ref[source, :, lanes],
                    place * parents - parents,
                )
            return carry

        lax.fori_loop(0, parents, per_box, 0)


def own_stage(place, index, offset, source, table, folded, turned, blocks, low, own, high):
    parents, columns, samples1 = turned.shape
    boxes, slots, rows, unknowns = blocks.shape
    children = boxes // parents
    hbm = pl.BlockSpec(memory_space=pl.ANY)
    return pl.pallas_call(
        own_kernel,
        grid=(parents,),
        out_shape=(
            jax.ShapeDtypeStruct((boxes, rows, columns), F32),
            jax.ShapeDtypeStruct((parents, columns, samples1), F32),
            jax.ShapeDtypeStruct((folded.shape[1], folded.shape[0]), BF16),
        ),
        in_specs=[smem()] * 4
        + [
            pl.BlockSpec(table.shape, lambda i: (0, 0)),
            pl.BlockSpec(folded.shape, lambda i: (0, 0)),
            pl.BlockSpec(turned.shape, lambda i: (0, 0, 0)),
            pl.BlockSpec((children, slots, rows, unknowns), lambda i: (i, 0, 0, 0)),
        ]
        + [hbm] * 3,
        out_specs=(
            pl.BlockSpec((children, rows, columns), lambda i: (i, 0, 0)),
            pl.BlockSpec((parents, columns, samples1), lambda i: (0, 0, 0)),
            pl.BlockSpec((folded.shape[1], folded.shape[0]), lambda i: (0, 0)),
        ),
        scratch_shapes=[
            pltpu.VMEM((3 * boxes, unknowns, columns), BF16),
            pltpu.VMEM((3 * parents, columns, samples1), F32),
            pltpu.VMEM((samples1 // 128, table.shape[0], 128), F32),
            pltpu.SemaphoreType.DMA((3,)),
        ],
        compiler_params=params(56),
        cost_estimate=cost(12 * 10**9, 20 * 2**20),
        name="own_stage",
    )(place, index, offset, source, table, folded, turned, blocks, low, own, high)


def other_kernel(
    place_ref, index_ref, blocks_ref, low_ref, own_ref, even_ref, odd_ref, near_ref, field_ref, sem,
    *, first,
):
    step = pl.program_id(0)
    start, wait = field_copies(place_ref[0], low_ref, own_ref, (even_ref, odd_ref), field_ref, sem)

    @pl.when(step == 0)
    def _():
        start()
        wait()

    near_rows(
        place_ref[0], index_ref, blocks_ref, field_ref, near_ref, first + step * blocks_ref.shape[0]
    )


def other_stage(place, index, blocks, low, own, even, odd, first, count, name):
    boxes, unknowns, columns = own.shape
    _, slots, rows, _ = blocks.shape
    chunk = min(8, count)
    hbm = pl.BlockSpec(memory_space=pl.ANY)
    return pl.pallas_call(
        functools.partial(other_kernel, first=first),
        grid=(count // chunk,),
        out_shape=jax.ShapeDtypeStruct((count, rows, columns), BF16),
        in_specs=[
            smem(),
            smem(),
            pl.BlockSpec((chunk, slots, rows, unknowns), lambda i: (first // chunk + i, 0, 0, 0)),
        ]
        + [hbm] * 4,
        out_specs=pl.BlockSpec((chunk, rows, columns), lambda i: (i, 0, 0)),
        scratch_shapes=[
            pltpu.VMEM((3 * boxes, unknowns, columns), BF16),
            pltpu.SemaphoreType.DMA((3,)),
        ],
        compiler_params=params(56),
        cost_estimate=cost(count * 10**8, 8 * 2**20 + count * 10**5),
        name=name,
    )(place, index, blocks, low, own, even, odd)


def down_kernel(
    place_ref, sigma_ref, inc_ref, two_ref, across_ref, unfold_ref, field_ref, near_ref,
    out_ref, flat_ref, local_ref, *, children, shifts, pair,
):
    chunks, columns, lanes = inc_ref.shape[1:]
    step = pl.program_id(0)

    @pl.when(step % children == 0)
    def _():
        for one in range(chunks):
            flat_ref[:, one * lanes : (one + 1) * lanes] = inc_ref[0, one]

    down = jnp.dot(flat_ref[...], two_ref[0], preferred_element_type=F32)
    local_ref[pl.ds((step % pair) * columns, columns), :] = (down + across_ref[0]).astype(BF16)

    @pl.when(step % pair == pair - 1)
    def _():
        far = lax.dot_general(unfold_ref[...], local_ref[...], NT, preferred_element_type=F32)
        boxes, unknowns, _ = out_ref.shape
        per = boxes // pair
        half = unknowns // 2
        re, im = sigma_ref[0, 0], sigma_ref[0, 1]
        for one in range(pair):
            mine = far[:, one * columns : (one + 1) * columns].reshape(per, unknowns, columns)
            span = slice(one * per, (one + 1) * per)
            real = field_ref[span, :half, :].astype(F32)
            imag = field_ref[span, half:, :].astype(F32)
            out_ref[span, :half, :] = mine[:, :half] - (re * real - im * imag)
            out_ref[span, half:, :] = mine[:, half:] - (re * imag + im * real)
        rows = near_ref.shape[1]
        for shift in range(shifts):

            @pl.when(place_ref[1] == shift)
            def _():
                out_ref[:, shift * rows : (shift + 1) * rows, :] += near_ref[...]


def downward(place, sigma, inc, interp_two, across, unfold, field, near_own, shifts):
    grand, chunks, columns, lanes = inc.shape
    children, samples2, samples1 = interp_two.shape
    boxes, unknowns, _ = field.shape
    rows = near_own.shape[1]
    pair = 2 if children % 2 == 0 else 1
    per = pair * (boxes // across.shape[0])
    return pl.pallas_call(
        functools.partial(down_kernel, children=children, shifts=shifts, pair=pair),
        grid=(grand * children,),
        out_shape=jax.ShapeDtypeStruct((boxes, unknowns, columns), F32),
        in_specs=[
            smem(),
            smem(),
            pl.BlockSpec((1, chunks, columns, lanes), lambda c: (c // children, 0, 0, 0)),
            pl.BlockSpec((1, samples2, samples1), lambda c: (c % children, 0, 0)),
            pl.BlockSpec((1, columns, samples1), lambda c: (c, 0, 0)),
            pl.BlockSpec(unfold.shape, lambda c: (0, 0)),
            pl.BlockSpec((per, unknowns, columns), lambda c: (c // pair, 0, 0)),
            pl.BlockSpec((per, rows, columns), lambda c: (c // pair, 0, 0)),
        ],
        out_specs=pl.BlockSpec((per, unknowns, columns), lambda c: (c // pair, 0, 0)),
        scratch_shapes=[
            pltpu.VMEM((columns, chunks * lanes), BF16),
            pltpu.VMEM((pair * columns, samples1), BF16),
        ],
        compiler_params=params(56),
        cost_estimate=cost(6 * 10**9, 30 * 2**20),
        name="downward",
    )(place, sigma, inc, interp_two, across, unfold, field, near_own)


def join_kernel(place_ref, total_ref, part_ref, out_ref):
    out_ref[...] = total_ref[...] + part_ref[...].astype(F32)


def join(place, total, part, first, name):
    boxes, unknowns, columns = total.shape
    count, rows, _ = part.shape
    step = min(16, count)
    half = pl.BlockSpec((step, rows, columns), lambda i, place_ref: (first // step + i, 1 - place_ref[1], 0))
    return pl.pallas_call(
        join_kernel,
        grid_spec=pltpu.PrefetchScalarGridSpec(
            num_scalar_prefetch=1,
            grid=(count // step,),
            in_specs=[half, pl.BlockSpec((step, rows, columns), lambda i, place_ref: (i, 0, 0))],
            out_specs=half,
        ),
        out_shape=jax.ShapeDtypeStruct(total.shape, F32),
        input_output_aliases={1: 0},
        compiler_params=params(8),
        cost_estimate=cost(10**7, 2 * 2**20),
        name=name,
    )(place, total, part)


def body(
    vectors, sigma, near_blocks, near_index, radiate, interp_one, interp_two, trans_one,
    level1_source, level1_offset, trans_two, level2_source, level2_offset,
):
    field = vectors[0]
    boxes, unknowns, columns = field.shape
    children, samples1, _ = interp_one.shape
    samples2 = interp_two.shape[1]
    parents = boxes // children
    grand = parents // children
    count = lax.axis_size("box")
    shifts = lax.axis_size("shift")
    place = jnp.stack([lax.axis_index("box"), lax.axis_index("shift")]).astype(jnp.int32)

    up = [(i, i + 1) for i in range(count - 1)]
    down = [(i + 1, i) for i in range(count - 1)]
    swap = [(s, shifts - 1 - s) for s in range(shifts)]
    pair_down = [(i + 1, i) for i in range(0, count - 1, 2)]
    odd_swap = [
        (i * shifts + s, i * shifts + shifts - 1 - s) for i in range(1, count, 2) for s in range(shifts)
    ]

    other = lax.ppermute(field, "shift", swap)
    high = lax.ppermute(field, "box", down)
    low = lax.ppermute(field, "box", up)

    folded, upper, turned = fold(
        interp_one, radiate, field.reshape(parents, children * unknowns, columns)
    )
    coarse = coarsen(interp_two, upper)
    chunk = samples2 // count
    pieces = coarse.reshape(grand, count, chunk, columns).swapaxes(0, 1)
    spread = lax.all_to_all(pieces, "box", split_axis=0, concat_axis=0, tiled=True)
    spread = spread.reshape(count * grand, chunk, columns)
    if chunk % 128 == 0:
        inc = done = level2(level2_offset, level2_source, trans_two, spread)
        inc = lax.all_to_all(
            inc.reshape(count, grand, columns, chunk), "box", split_axis=0, concat_axis=0, tiled=True
        ).swapaxes(0, 1)
    else:
        inc = done = weighted_lists(spread, trans_two, level2_offset, level2_source).astype(BF16)
        inc = lax.all_to_all(
            inc.reshape(count, grand, chunk, columns), "box", split_axis=0, concat_axis=0, tiled=True
        ).swapaxes(0, 1)
        inc = inc.reshape(grand, samples2 // 128, 128, columns).swapaxes(2, 3)

    low, high, other, _ = lax.optimization_barrier((low, high, other, done))
    high_odd = lax.ppermute(high, ("box", "shift"), odd_swap)
    low_other = lax.ppermute(other, "box", up)
    high_even = lax.ppermute(other, "box", pair_down)

    index = near_index.T
    near_own, across, unfold = own_stage(
        place, index, level1_offset, level1_source, trans_one, folded, turned, near_blocks,
        low, field, high,
    )
    splits = 2
    part = boxes // splits
    arrived = []
    for one in range(splits):
        mine = other_stage(
            place, index, near_blocks, low_other, other, high_even, high_odd,
            one * part, part, "other_stage" + str(one),
        )
        arrived.append(lax.ppermute(mine, "shift", swap))

    total = downward(place, sigma, inc, interp_two, across, unfold, field, near_own, shifts)
    for one in range(splits):
        total = join(place, total, arrived[one], one * part, "join" + str(one))
    return total[None]


def solution(mesh):
    in_specs = (
        P("shift", "box", None, None),
        P("shift", None),
        P("box", None, "shift", None),
        P("box", None),
        P(),
        P(),
        P(),
        P(),
        P("box", None),
        P("box", None),
        P(None, "box"),
        P(),
        P(),
    )
    out_specs = P("shift", "box", None, None)
    return jax.shard_map(body, mesh=mesh, in_specs=in_specs, out_specs=out_specs, check_vma=False)
```

```python
import functools

import jax
import jax.numpy as jnp
from jax import lax
from jax.experimental import pallas as pl
from jax.experimental.pallas import tpu as pltpu
from jax.sharding import PartitionSpec as P


F32 = jnp.float32
BF16 = jnp.bfloat16
NT = (((1,), (1,)), ((), ()))


def vmem():
    return pl.BlockSpec(memory_space=pltpu.VMEM)


def smem():
    return pl.BlockSpec(memory_space=pltpu.SMEM)


def cost(flops, moved):
    return pl.CostEstimate(flops=flops, bytes_accessed=moved, transcendentals=0)


def params(mib):
    return pltpu.CompilerParams(vmem_limit_bytes=mib << 20)


def fold_kernel(one_ref, radiate_ref, field_ref, fold_ref, upper_ref, turned_ref):
    children, samples1, _ = one_ref.shape
    unknowns = radiate_ref.shape[1]
    pair, _, columns = field_ref.shape

    @pl.when(pl.program_id(0) == 0)
    def _():
        for child in range(children):
            fold_ref[:, child * unknowns : (child + 1) * unknowns] = jnp.dot(
                one_ref[child], radiate_ref[...], preferred_element_type=F32
            ).astype(BF16)

    wide = jnp.concatenate([field_ref[one] for one in range(pair)], axis=1)
    pattern = jnp.dot(fold_ref[...], wide, preferred_element_type=F32)
    for one in range(pair):
        mine = pattern[:, one * columns : (one + 1) * columns]
        upper_ref[one] = mine.astype(BF16)
        turned_ref[one] = mine.T.astype(BF16)


def fold(interp_one, radiate, field):
    children, samples1, samples0 = interp_one.shape
    unknowns = radiate.shape[1]
    parents, width, columns = field.shape
    pair = 2 if parents % 2 == 0 else 1
    return pl.pallas_call(
        fold_kernel,
        grid=(parents // pair,),
        out_shape=(
            jax.ShapeDtypeStruct((samples1, children * unknowns), BF16),
            jax.ShapeDtypeStruct((parents, samples1, columns), BF16),
            jax.ShapeDtypeStruct((parents, columns, samples1), BF16),
        ),
        in_specs=[
            pl.BlockSpec(interp_one.shape, lambda i: (0, 0, 0)),
            pl.BlockSpec(radiate.shape, lambda i: (0, 0)),
            pl.BlockSpec((pair, width, columns), lambda i: (i, 0, 0)),
        ],
        out_specs=(
            pl.BlockSpec((samples1, children * unknowns), lambda i: (0, 0)),
            pl.BlockSpec((pair, samples1, columns), lambda i: (i, 0, 0)),
            pl.BlockSpec((pair, columns, samples1), lambda i: (i, 0, 0)),
        ),
        compiler_params=params(56),
        cost_estimate=cost(3 * 10**9, 6 * 2**20),
        name="fold",
    )(interp_one, radiate, field)


def coarse_kernel(two_ref, upper_ref, out_ref):
    total = jnp.dot(two_ref[0], upper_ref[0], preferred_element_type=F32)
    for child in range(1, two_ref.shape[0]):
        total += jnp.dot(two_ref[child], upper_ref[child], preferred_element_type=F32)
    out_ref[0] = total.astype(BF16)


def coarsen(interp_two, upper):
    children, samples2, samples1 = interp_two.shape
    parents, _, columns = upper.shape
    grand = parents // children
    rows = min(samples2, 256)
    return pl.pallas_call(
        coarse_kernel,
        grid=(samples2 // rows, grand),
        out_shape=jax.ShapeDtypeStruct((grand, samples2, columns), BF16),
        in_specs=[
            pl.BlockSpec((children, rows, samples1), lambda q, g: (0, q, 0)),
            pl.BlockSpec((children, samples1, columns), lambda q, g: (g, 0, 0)),
        ],
        out_specs=pl.BlockSpec((1, rows, columns), lambda q, g: (g, q, 0)),
        compiler_params=params(56),
        cost_estimate=cost(4 * 10**9, 18 * 2**20),
        name="coarsen",
    )(interp_two, upper)


def live_count(source_ref, row):
    total = jnp.int32(0)
    for slot in range(source_ref.shape[1]):
        total += (source_ref[row, slot] >= 0).astype(jnp.int32)
    return total


def list_sum(offset_ref, source_ref, box, shape, weight_at, pattern_at, base):
    unroll = next(n for n in (4, 2, 1) if source_ref.shape[1] % n == 0)

    def add(trip, total):
        for one in range(unroll):
            slot = trip * unroll + one
            named = source_ref[box, slot]
            live = named >= 0
            weight = weight_at(offset_ref[box, slot]) * live.astype(F32)
            total = total + weight * pattern_at(jnp.where(live, named - base, 0))
        return total

    trips = (live_count(source_ref, box) + unroll - 1) // unroll
    return lax.fori_loop(0, trips, add, jnp.zeros(shape, F32))


def level2_kernel(offset_ref, source_ref, table_ref, pattern_ref, out_ref, turned_ref):
    boxes = pattern_ref.shape[0]

    def turn(box, carry):
        turned_ref[box] = pattern_ref[box].astype(F32).T
        return carry

    lax.fori_loop(0, boxes, turn, 0)

    def per_box(box, carry):
        total = list_sum(
            offset_ref, source_ref, box, turned_ref.shape[1:],
            lambda offset: table_ref[pl.ds(offset, 1), :], lambda source: turned_ref[source], 0,
        )
        out_ref[box] = total.astype(BF16)
        return carry

    lax.fori_loop(0, out_ref.shape[0], per_box, 0)


def level2(offset, source, table, pattern):
    boxes, samples, columns = pattern.shape
    return pl.pallas_call(
        level2_kernel,
        out_shape=jax.ShapeDtypeStruct((offset.shape[0], columns, samples), BF16),
        in_specs=[smem(), smem(), vmem(), vmem()],
        out_specs=vmem(),
        scratch_shapes=[pltpu.VMEM((boxes, columns, samples), F32)],
        compiler_params=params(8),
        cost_estimate=cost(3 * 10**9, 2 * 2**20),
        name="level2",
    )(offset, source, table, pattern)


def weighted_lists(pattern, table, offsets, sources):
    live = sources >= 0
    weights = table[offsets] * live[:, :, None].astype(F32)
    picked = pattern[jnp.where(live, sources, 0)]
    return jnp.einsum("cjk,cjkr->ckr", weights, picked, preferred_element_type=F32)


def field_copies(place, low_ref, own_ref, high_refs, field_ref, sem):
    boxes = own_ref.shape[0]

    def into(ref, which):
        return pltpu.make_async_copy(ref, field_ref.at[pl.ds(which * boxes, boxes)], sem.at[which])

    def start():
        into(low_ref, 0).start()
        into(own_ref, 1).start()
        for which, ref in enumerate(high_refs):

            @pl.when(place % len(high_refs) == which)
            def _():
                into(ref, 2).start()

    def wait():
        into(low_ref, 0).wait()
        into(own_ref, 1).wait()
        into(high_refs[0], 2).wait()

    return start, wait


def near_rows(place, index_ref, blocks_ref, field_ref, out_ref, row):
    boxes = field_ref.shape[0] // 3
    chunk, slots = blocks_ref.shape[:2]
    base = place * boxes - boxes
    for box in range(chunk):
        total = None
        for slot in range(0, slots, 2):
            left, right = [], []
            for one in range(slot, min(slot + 2, slots)):
                block = blocks_ref[box, one]
                if one == 0:
                    where = boxes + row + box
                else:
                    named = index_ref[one, row + box]
                    live = named >= 0
                    where = jnp.where(live, named - base, boxes)
                    block = jnp.where(live, block, jnp.zeros_like(block))
                left.append(block)
                right.append(field_ref[where])
            part = jnp.dot(
                jnp.concatenate(left, axis=1),
                jnp.concatenate(right, axis=0),
                preferred_element_type=F32,
            )
            total = part if total is None else total + part
        out_ref[box] = total.astype(out_ref.dtype)


def own_kernel(
    place_ref, index_ref, offset_ref, source_ref, table_ref, fold_ref, turned_ref, blocks_ref,
    low_ref, own_ref, high_ref, near_ref, across_ref, unfold_ref,
    field_ref, rim_ref, rows_ref, sem,
):
    step = pl.program_id(0)
    parents, columns, samples1 = turned_ref.shape
    children = blocks_ref.shape[0]
    boxes = own_ref.shape[0]
    unknowns = field_ref.shape[1]
    width = rows_ref.shape[2]
    place = place_ref[0]
    start, wait = field_copies(place, low_ref, own_ref, (high_ref,), field_ref, sem)

    @pl.when(step == 0)
    def _():
        start()
        for part in range(rows_ref.shape[0]):
            rows_ref[part] = table_ref[:, part * width : (part + 1) * width]
        for first in range(0, fold_ref.shape[1], 128):
            unfold_ref[first : first + 128, :] = fold_ref[:, first : first + 128].T
        for parent in range(parents):
            rim_ref[parents + parent] = turned_ref[parent].astype(F32)
        wait()

    near_rows(place, index_ref, blocks_ref, field_ref, near_ref, step * children)
    low = field_ref[pl.ds(step * children, children)].reshape(children * unknowns, columns)
    high = field_ref[pl.ds(2 * boxes + step * children, children)].reshape(children * unknowns, columns)
    both = jnp.dot(
        fold_ref[...], jnp.concatenate([low, high], axis=1), preferred_element_type=F32
    )
    rim_ref[step] = both[:, :columns].T.astype(BF16).astype(F32)
    rim_ref[2 * parents + step] = both[:, columns:].T.astype(BF16).astype(F32)

    @pl.when(step == parents - 1)
    def _():
        def per_box(box, carry):
            for part in range(samples1 // width):
                lanes = slice(part * width, (part + 1) * width)
                across_ref[box, :, lanes] = list_sum(
                    offset_ref, source_ref, box, (columns, width),
                    lambda offset: rows_ref[part, pl.ds(offset, 1), :],
                    lambda source: rim_ref[source, :, lanes],
                    place * parents - parents,
                )
            return carry

        lax.fori_loop(0, parents, per_box, 0)


def own_stage(place, index, offset, source, table, folded, turned, blocks, low, own, high):
    parents, columns, samples1 = turned.shape
    boxes, slots, rows, unknowns = blocks.shape
    children = boxes // parents
    hbm = pl.BlockSpec(memory_space=pl.ANY)
    return pl.pallas_call(
        own_kernel,
        grid=(parents,),
        out_shape=(
            jax.ShapeDtypeStruct((boxes, rows, columns), F32),
            jax.ShapeDtypeStruct((parents, columns, samples1), F32),
            jax.ShapeDtypeStruct((folded.shape[1], folded.shape[0]), BF16),
        ),
        in_specs=[smem()] * 4
        + [
            pl.BlockSpec(table.shape, lambda i: (0, 0)),
            pl.BlockSpec(folded.shape, lambda i: (0, 0)),
            pl.BlockSpec(turned.shape, lambda i: (0, 0, 0)),
            pl.BlockSpec((children, slots, rows, unknowns), lambda i: (i, 0, 0, 0)),
        ]
        + [hbm] * 3,
        out_specs=(
            pl.BlockSpec((children, rows, columns), lambda i: (i, 0, 0)),
            pl.BlockSpec((parents, columns, samples1), lambda i: (0, 0, 0)),
            pl.BlockSpec((folded.shape[1], folded.shape[0]), lambda i: (0, 0)),
        ),
        scratch_shapes=[
            pltpu.VMEM((3 * boxes, unknowns, columns), BF16),
            pltpu.VMEM((3 * parents, columns, samples1), F32),
            pltpu.VMEM((samples1 // 128, table.shape[0], 128), F32),
            pltpu.SemaphoreType.DMA((3,)),
        ],
        compiler_params=params(56),
        cost_estimate=cost(12 * 10**9, 20 * 2**20),
        name="own_stage",
    )(place, index, offset, source, table, folded, turned, blocks, low, own, high)


def other_kernel(
    place_ref, index_ref, blocks_ref, low_ref, own_ref, even_ref, odd_ref, near_ref, field_ref, sem,
    *, first,
):
    step = pl.program_id(0)
    start, wait = field_copies(place_ref[0], low_ref, own_ref, (even_ref, odd_ref), field_ref, sem)

    @pl.when(step == 0)
    def _():
        start()
        wait()

    near_rows(
        place_ref[0], index_ref, blocks_ref, field_ref, near_ref, first + step * blocks_ref.shape[0]
    )


def other_stage(place, index, blocks, low, own, even, odd, first, count, name):
    boxes, unknowns, columns = own.shape
    _, slots, rows, _ = blocks.shape
    chunk = min(8, count)
    hbm = pl.BlockSpec(memory_space=pl.ANY)
    return pl.pallas_call(
        functools.partial(other_kernel, first=first),
        grid=(count // chunk,),
        out_shape=jax.ShapeDtypeStruct((count, rows, columns), BF16),
        in_specs=[
            smem(),
            smem(),
            pl.BlockSpec((chunk, slots, rows, unknowns), lambda i: (first // chunk + i, 0, 0, 0)),
        ]
        + [hbm] * 4,
        out_specs=pl.BlockSpec((chunk, rows, columns), lambda i: (i, 0, 0)),
        scratch_shapes=[
            pltpu.VMEM((3 * boxes, unknowns, columns), BF16),
            pltpu.SemaphoreType.DMA((3,)),
        ],
        compiler_params=params(56),
        cost_estimate=cost(count * 10**8, 8 * 2**20 + count * 10**5),
        name=name,
    )(place, index, blocks, low, own, even, odd)


def down_kernel(
    place_ref, sigma_ref, inc_ref, two_ref, across_ref, unfold_ref, field_ref, near_ref,
    out_ref, flat_ref, local_ref, *, children, shifts, pair,
):
    chunks, columns, lanes = inc_ref.shape[1:]
    step = pl.program_id(0)

    @pl.when(step % children == 0)
    def _():
        for one in range(chunks):
            flat_ref[:, one * lanes : (one + 1) * lanes] = inc_ref[0, one]

    down = jnp.dot(flat_ref[...], two_ref[0], preferred_element_type=F32)
    local_ref[pl.ds((step % pair) * columns, columns), :] = (down + across_ref[0]).astype(BF16)

    @pl.when(step % pair == pair - 1)
    def _():
        far = lax.dot_general(unfold_ref[...], local_ref[...], NT, preferred_element_type=F32)
        boxes, unknowns, _ = out_ref.shape
        per = boxes // pair
        half = unknowns // 2
        re, im = sigma_ref[0, 0], sigma_ref[0, 1]
        for one in range(pair):
            mine = far[:, one * columns : (one + 1) * columns].reshape(per, unknowns, columns)
            span = slice(one * per, (one + 1) * per)
            real = field_ref[span, :half, :].astype(F32)
            imag = field_ref[span, half:, :].astype(F32)
            out_ref[span, :half, :] = mine[:, :half] - (re * real - im * imag)
            out_ref[span, half:, :] = mine[:, half:] - (re * imag + im * real)
        rows = near_ref.shape[1]
        for shift in range(shifts):

            @pl.when(place_ref[1] == shift)
            def _():
                out_ref[:, shift * rows : (shift + 1) * rows, :] += near_ref[...]


def downward(place, sigma, inc, interp_two, across, unfold, field, near_own, shifts):
    grand, chunks, columns, lanes = inc.shape
    children, samples2, samples1 = interp_two.shape
    boxes, unknowns, _ = field.shape
    rows = near_own.shape[1]
    pair = 2 if children % 2 == 0 else 1
    per = pair * (boxes // across.shape[0])
    return pl.pallas_call(
        functools.partial(down_kernel, children=children, shifts=shifts, pair=pair),
        grid=(grand * children,),
        out_shape=jax.ShapeDtypeStruct((boxes, unknowns, columns), F32),
        in_specs=[
            smem(),
            smem(),
            pl.BlockSpec((1, chunks, columns, lanes), lambda c: (c // children, 0, 0, 0)),
            pl.BlockSpec((1, samples2, samples1), lambda c: (c % children, 0, 0)),
            pl.BlockSpec((1, columns, samples1), lambda c: (c, 0, 0)),
            pl.BlockSpec(unfold.shape, lambda c: (0, 0)),
            pl.BlockSpec((per, unknowns, columns), lambda c: (c // pair, 0, 0)),
            pl.BlockSpec((per, rows, columns), lambda c: (c // pair, 0, 0)),
        ],
        out_specs=pl.BlockSpec((per, unknowns, columns), lambda c: (c // pair, 0, 0)),
        scratch_shapes=[
            pltpu.VMEM((columns, chunks * lanes), BF16),
            pltpu.VMEM((pair * columns, samples1), BF16),
        ],
        compiler_params=params(56),
        cost_estimate=cost(6 * 10**9, 30 * 2**20),
        name="downward",
    )(place, sigma, inc, interp_two, across, unfold, field, near_own)


def join_kernel(place_ref, total_ref, part_ref, out_ref):
    out_ref[...] = total_ref[...] + part_ref[...].astype(F32)


def join(place, total, part, first, name):
    boxes, unknowns, columns = total.shape
    count, rows, _ = part.shape
    step = min(16, count)
    half = pl.BlockSpec((step, rows, columns), lambda i, place_ref: (first // step + i, 1 - place_ref[1], 0))
    return pl.pallas_call(
        join_kernel,
        grid_spec=pltpu.PrefetchScalarGridSpec(
            num_scalar_prefetch=1,
            grid=(count // step,),
            in_specs=[half, pl.BlockSpec((step, rows, columns), lambda i, place_ref: (i, 0, 0))],
            out_specs=half,
        ),
        out_shape=jax.ShapeDtypeStruct(total.shape, F32),
        input_output_aliases={1: 0},
        compiler_params=params(8),
        cost_estimate=cost(10**7, 2 * 2**20),
        name=name,
    )(place, total, part)


def body(
    vectors, sigma, near_blocks, near_index, radiate, interp_one, interp_two, trans_one,
    level1_source, level1_offset, trans_two, level2_source, level2_offset,
):
    field = vectors[0]
    boxes, unknowns, columns = field.shape
    children, samples1, _ = interp_one.shape
    samples2 = interp_two.shape[1]
    parents = boxes // children
    grand = parents // children
    count = lax.axis_size("box")
    shifts = lax.axis_size("shift")
    place = jnp.stack([lax.axis_index("box"), lax.axis_index("shift")]).astype(jnp.int32)

    up = [(i, i + 1) for i in range(count - 1)]
    down = [(i + 1, i) for i in range(count - 1)]
    swap = [(s, shifts - 1 - s) for s in range(shifts)]
    pair_down = [(i + 1, i) for i in range(0, count - 1, 2)]
    odd_swap = [
        (i * shifts + s, i * shifts + shifts - 1 - s) for i in range(1, count, 2) for s in range(shifts)
    ]

    other = lax.ppermute(field, "shift", swap)
    high = lax.ppermute(field, "box", down)

    folded, upper, turned = fold(
        interp_one, radiate, field.reshape(parents, children * unknowns, columns)
    )
    coarse = coarsen(interp_two, upper)
    coarse, late = lax.optimization_barrier((coarse, field))
    low = lax.ppermute(late, "box", up)
    chunk = samples2 // count
    pieces = coarse.reshape(grand, count, chunk, columns).swapaxes(0, 1)
    spread = lax.all_to_all(pieces, "box", split_axis=0, concat_axis=0, tiled=True)
    spread = spread.reshape(count * grand, chunk, columns)
    if chunk % 128 == 0:
        inc = level2(level2_offset, level2_source, trans_two, spread)
        inc = lax.all_to_all(
            inc.reshape(count, grand, columns, chunk), "box", split_axis=0, concat_axis=0, tiled=True
        ).swapaxes(0, 1)
    else:
        inc = weighted_lists(spread, trans_two, level2_offset, level2_source).astype(BF16)
        inc = lax.all_to_all(
            inc.reshape(count, grand, chunk, columns), "box", split_axis=0, concat_axis=0, tiled=True
        ).swapaxes(0, 1)
        inc = inc.reshape(grand, samples2 // 128, 128, columns).swapaxes(2, 3)

    high_odd = lax.ppermute(high, ("box", "shift"), odd_swap)
    low_other = lax.ppermute(other, "box", up)
    high_even = lax.ppermute(other, "box", pair_down)

    index = near_index.T
    near_own, across, unfold = own_stage(
        place, index, level1_offset, level1_source, trans_one, folded, turned, near_blocks,
        low, field, high,
    )
    splits = 2
    part = boxes // splits
    arrived = []
    for one in range(splits):
        mine = other_stage(
            place, index, near_blocks, low_other, other, high_even, high_odd,
            one * part, part, "other_stage" + str(one),
        )
        arrived.append(lax.ppermute(mine, "shift", swap))

    total = downward(place, sigma, inc, interp_two, across, unfold, field, near_own, shifts)
    for one in range(splits):
        total = join(place, total, arrived[one], one * part, "join" + str(one))
    return total[None]


def solution(mesh):
    in_specs = (
        P("shift", "box", None, None),
        P("shift", None),
        P("box", None, "shift", None),
        P("box", None),
        P(),
        P(),
        P(),
        P(),
        P("box", None),
        P("box", None),
        P(None, "box"),
        P(),
        P(),
    )
    out_specs = P("shift", "box", None, None)
    return jax.shard_map(body, mesh=mesh, in_specs=in_specs, out_specs=out_specs, check_vma=False)
```

```python
import functools

import jax
import jax.numpy as jnp
from jax import lax
from jax.experimental import pallas as pl
from jax.experimental.pallas import tpu as pltpu
from jax.sharding import PartitionSpec as P


F32 = jnp.float32
BF16 = jnp.bfloat16
NT = (((1,), (1,)), ((), ()))


def vmem():
    return pl.BlockSpec(memory_space=pltpu.VMEM)


def smem():
    return pl.BlockSpec(memory_space=pltpu.SMEM)


def cost(flops, moved):
    return pl.CostEstimate(flops=flops, bytes_accessed=moved, transcendentals=0)


def params(mib):
    return pltpu.CompilerParams(vmem_limit_bytes=mib << 20)


def fold_kernel(one_ref, radiate_ref, field_ref, fold_ref, upper_ref, turned_ref):
    children, _, _ = one_ref.shape
    unknowns = radiate_ref.shape[1]
    pair, _, columns = field_ref.shape

    @pl.when(pl.program_id(0) == 0)
    def _():
        for child in range(children):
            fold_ref[:, child * unknowns : (child + 1) * unknowns] = jnp.dot(
                one_ref[child], radiate_ref[...], preferred_element_type=F32
            ).astype(BF16)

    wide = jnp.concatenate([field_ref[one] for one in range(pair)], axis=1)
    pattern = jnp.dot(fold_ref[...], wide, preferred_element_type=F32)
    for one in range(pair):
        mine = pattern[:, one * columns : (one + 1) * columns]
        upper_ref[one] = mine.astype(BF16)
        turned_ref[one] = mine.T.astype(BF16)


def fold(interp_one, radiate, field):
    children, samples1, _ = interp_one.shape
    unknowns = radiate.shape[1]
    parents, width, columns = field.shape
    pair = 2 if parents % 2 == 0 else 1
    return pl.pallas_call(
        fold_kernel,
        grid=(parents // pair,),
        out_shape=(
            jax.ShapeDtypeStruct((samples1, children * unknowns), BF16),
            jax.ShapeDtypeStruct((parents, samples1, columns), BF16),
            jax.ShapeDtypeStruct((parents, columns, samples1), BF16),
        ),
        in_specs=[
            pl.BlockSpec(interp_one.shape, lambda i: (0, 0, 0)),
            pl.BlockSpec(radiate.shape, lambda i: (0, 0)),
            pl.BlockSpec((pair, width, columns), lambda i: (i, 0, 0)),
        ],
        out_specs=(
            pl.BlockSpec((samples1, children * unknowns), lambda i: (0, 0)),
            pl.BlockSpec((pair, samples1, columns), lambda i: (i, 0, 0)),
            pl.BlockSpec((pair, columns, samples1), lambda i: (i, 0, 0)),
        ),
        compiler_params=params(56),
        cost_estimate=cost(3 * 10**9, 6 * 2**20),
        name="fold",
    )(interp_one, radiate, field)


def coarse_kernel(two_ref, upper_ref, out_ref):
    total = jnp.dot(two_ref[0], upper_ref[0], preferred_element_type=F32)
    for child in range(1, two_ref.shape[0]):
        total += jnp.dot(two_ref[child], upper_ref[child], preferred_element_type=F32)
    out_ref[0] = total.astype(BF16)


def coarsen(interp_two, upper):
    children, samples2, samples1 = interp_two.shape
    parents, _, columns = upper.shape
    grand = parents // children
    rows = min(samples2, 256)
    return pl.pallas_call(
        coarse_kernel,
        grid=(samples2 // rows, grand),
        out_shape=jax.ShapeDtypeStruct((grand, samples2, columns), BF16),
        in_specs=[
            pl.BlockSpec((children, rows, samples1), lambda q, g: (0, q, 0)),
            pl.BlockSpec((children, samples1, columns), lambda q, g: (g, 0, 0)),
        ],
        out_specs=pl.BlockSpec((1, rows, columns), lambda q, g: (g, q, 0)),
        compiler_params=params(56),
        cost_estimate=cost(4 * 10**9, 18 * 2**20),
        name="coarsen",
    )(interp_two, upper)


def live_count(source_ref, row):
    total = jnp.int32(0)
    for slot in range(source_ref.shape[1]):
        total += (source_ref[row, slot] >= 0).astype(jnp.int32)
    return total


def list_sum(offset_ref, source_ref, box, shape, weight_at, pattern_at, base):
    unroll = next(n for n in (4, 2, 1) if source_ref.shape[1] % n == 0)

    def add(trip, total):
        for one in range(unroll):
            slot = trip * unroll + one
            named = source_ref[box, slot]
            live = named >= 0
            weight = weight_at(offset_ref[box, slot]) * live.astype(F32)
            total = total + weight * pattern_at(jnp.where(live, named - base, 0))
        return total

    trips = (live_count(source_ref, box) + unroll - 1) // unroll
    return lax.fori_loop(0, trips, add, jnp.zeros(shape, F32))


def level2_kernel(offset_ref, source_ref, table_ref, pattern_ref, out_ref, turned_ref):
    boxes = pattern_ref.shape[0]

    def turn(box, carry):
        turned_ref[box] = pattern_ref[box].astype(F32).T
        return carry

    lax.fori_loop(0, boxes, turn, 0)

    def per_box(box, carry):
        total = list_sum(
            offset_ref, source_ref, box, turned_ref.shape[1:],
            lambda offset: table_ref[pl.ds(offset, 1), :], lambda source: turned_ref[source], 0,
        )
        out_ref[box] = total.astype(BF16)
        return carry

    lax.fori_loop(0, out_ref.shape[0], per_box, 0)


def level2(offset, source, table, pattern):
    boxes, samples, columns = pattern.shape
    return pl.pallas_call(
        level2_kernel,
        out_shape=jax.ShapeDtypeStruct((offset.shape[0], columns, samples), BF16),
        in_specs=[smem(), smem(), vmem(), vmem()],
        out_specs=vmem(),
        scratch_shapes=[pltpu.VMEM((boxes, columns, samples), F32)],
        compiler_params=params(8),
        cost_estimate=cost(3 * 10**9, 2 * 2**20),
        name="level2",
    )(offset, source, table, pattern)


def weighted_lists(pattern, table, offsets, sources):
    live = sources >= 0
    weights = table[offsets] * live[:, :, None].astype(F32)
    picked = pattern[jnp.where(live, sources, 0)]
    return jnp.einsum("cjk,cjkr->ckr", weights, picked, preferred_element_type=F32)


def level1_kernel(
    place_ref, offset_ref, source_ref, table_ref, fold_ref, turned_ref, low_ref, high_ref,
    across_ref, unfold_ref, rim_ref, rows_ref,
):
    step = pl.program_id(0)
    parents, columns, samples1 = turned_ref.shape
    width = rows_ref.shape[2]
    both = jnp.dot(
        fold_ref[...],
        jnp.concatenate([low_ref[0], high_ref[0]], axis=1),
        preferred_element_type=F32,
    )
    rim_ref[step] = both[:, :columns].T.astype(BF16).astype(F32)
    rim_ref[parents + step] = turned_ref[step].astype(F32)
    rim_ref[2 * parents + step] = both[:, columns:].T.astype(BF16).astype(F32)

    @pl.when(step == 0)
    def _():
        for part in range(rows_ref.shape[0]):
            rows_ref[part] = table_ref[:, part * width : (part + 1) * width]
        for first in range(0, fold_ref.shape[1], 128):
            unfold_ref[first : first + 128, :] = fold_ref[:, first : first + 128].T

    @pl.when(step == parents - 1)
    def _():
        def per_box(box, carry):
            for part in range(samples1 // width):
                lanes = slice(part * width, (part + 1) * width)
                across_ref[box, :, lanes] = list_sum(
                    offset_ref, source_ref, box, (columns, width),
                    lambda offset: rows_ref[part, pl.ds(offset, 1), :],
                    lambda source: rim_ref[source, :, lanes],
                    place_ref[0] * parents - parents,
                )
            return carry

        lax.fori_loop(0, parents, per_box, 0)


def level1(place, offset, source, table, folded, turned, low, high):
    parents, columns, samples1 = turned.shape
    around = pl.BlockSpec((1,) + low.shape[1:], lambda i: (i, 0, 0))
    return pl.pallas_call(
        level1_kernel,
        grid=(parents,),
        out_shape=(
            jax.ShapeDtypeStruct((parents, columns, samples1), F32),
            jax.ShapeDtypeStruct((folded.shape[1], folded.shape[0]), BF16),
        ),
        in_specs=[smem()] * 3
        + [
            pl.BlockSpec(table.shape, lambda i: (0, 0)),
            pl.BlockSpec(folded.shape, lambda i: (0, 0)),
            pl.BlockSpec(turned.shape, lambda i: (0, 0, 0)),
            around,
            around,
        ],
        out_specs=(
            pl.BlockSpec((parents, columns, samples1), lambda i: (0, 0, 0)),
            pl.BlockSpec((folded.shape[1], folded.shape[0]), lambda i: (0, 0)),
        ),
        scratch_shapes=[
            pltpu.VMEM((3 * parents, columns, samples1), F32),
            pltpu.VMEM((samples1 // 128, table.shape[0], 128), F32),
        ],
        compiler_params=params(56),
        cost_estimate=cost(8 * 10**9, 14 * 2**20),
        name="level1",
    )(place, offset, source, table, folded, turned, low, high)


def near_kernel(
    place_ref, index_ref, blocks_ref, low_ref, own_ref, high_ref,
    low_other_ref, other_ref, even_ref, odd_ref, mine_ref, theirs_ref, field_ref, sem,
    *, first, count,
):
    step = pl.program_id(0)
    place = place_ref[0]
    boxes, _, columns = own_ref.shape
    chunk, slots = blocks_ref.shape[:2]
    spans = ((first, boxes - first, 0), (0, boxes, 1), (0, first + count, 2))

    def into(ref, side, which):
        start, length, block = spans[which]
        return pltpu.make_async_copy(
            ref.at[pl.ds(start, length)],
            field_ref.at[
                pl.ds(block * boxes + start, length), :, pl.ds(side * columns, columns)
            ],
            sem.at[side, which],
        )

    @pl.when(step == 0)
    def _():
        for which, ref in enumerate((low_ref, own_ref, high_ref)):
            into(ref, 0, which).start()
        into(low_other_ref, 1, 0).start()
        into(other_ref, 1, 1).start()
        for parity, ref in enumerate((even_ref, odd_ref)):

            @pl.when(place % 2 == parity)
            def _():
                into(ref, 1, 2).start()

        for side, refs in enumerate(
            ((low_ref, own_ref, high_ref), (low_other_ref, other_ref, even_ref))
        ):
            for which, ref in enumerate(refs):
                into(ref, side, which).wait()

    base = place * boxes - boxes
    for box in range(chunk):
        row = first + step * chunk + box
        total = None
        for slot in range(0, slots, 2):
            left, right = [], []
            for one in range(slot, min(slot + 2, slots)):
                block = blocks_ref[box, one]
                if one == 0:
                    where = boxes + row
                else:
                    named = index_ref[one, row]
                    live = named >= 0
                    where = jnp.where(live, named - base, boxes)
                    block = jnp.where(live, block, jnp.zeros_like(block))
                left.append(block)
                right.append(field_ref[where])
            part = jnp.dot(
                jnp.concatenate(left, axis=1),
                jnp.concatenate(right, axis=0),
                preferred_element_type=F32,
            )
            total = part if total is None else total + part
        mine_ref[box] = total[:, :columns]
        theirs_ref[box] = total[:, columns:].astype(BF16)


def near(place, index, blocks, low, own, high, low_other, other, even, odd, first, count):
    boxes, unknowns, columns = own.shape
    _, slots, rows, _ = blocks.shape
    chunk = min(8, count)
    hbm = pl.BlockSpec(memory_space=pl.ANY)
    return pl.pallas_call(
        functools.partial(near_kernel, first=first, count=count),
        grid=(count // chunk,),
        out_shape=(
            jax.ShapeDtypeStruct((count, rows, columns), F32),
            jax.ShapeDtypeStruct((count, rows, columns), BF16),
        ),
        in_specs=[
            smem(),
            smem(),
            pl.BlockSpec((chunk, slots, rows, unknowns), lambda i: (first // chunk + i, 0, 0, 0)),
        ]
        + [hbm] * 7,
        out_specs=(pl.BlockSpec((chunk, rows, columns), lambda i: (i, 0, 0)),) * 2,
        scratch_shapes=[
            pltpu.VMEM((3 * boxes, unknowns, 2 * columns), BF16),
            pltpu.SemaphoreType.DMA((2, 3)),
        ],
        compiler_params=params(56),
        cost_estimate=cost(count * 2 * 10**8, 14 * 2**20 + count * 10**5),
    )(place, index, blocks, low, own, high, low_other, other, even, odd)


def part_index(which, per):
    return lambda i: (jnp.clip(i - which * per, 0, per - 1), 0, 0)


def down_kernel(place_ref, sigma_ref, inc_ref, two_ref, across_ref, unfold_ref, field_ref, *rest, children, pair, parts, shifts):
    near_refs, (out_ref, flat_ref, local_ref) = rest[:parts], rest[parts:]
    chunks, columns, lanes = inc_ref.shape[1:]
    step = pl.program_id(0)
    span_of = pl.num_programs(0) // parts

    @pl.when(step % children == 0)
    def _():
        for one in range(chunks):
            flat_ref[:, one * lanes : (one + 1) * lanes] = inc_ref[0, one]

    down = jnp.dot(flat_ref[...], two_ref[0], preferred_element_type=F32)
    local_ref[pl.ds((step % pair) * columns, columns), :] = (down + across_ref[0]).astype(BF16)

    @pl.when(step % pair == pair - 1)
    def _():
        far = lax.dot_general(unfold_ref[...], local_ref[...], NT, preferred_element_type=F32)
        boxes, unknowns, _ = out_ref.shape
        per = boxes // pair
        half = unknowns // 2
        re, im = sigma_ref[0, 0], sigma_ref[0, 1]
        for one in range(pair):
            mine = far[:, one * columns : (one + 1) * columns].reshape(per, unknowns, columns)
            span = slice(one * per, (one + 1) * per)
            real = field_ref[span, :half, :].astype(F32)
            imag = field_ref[span, half:, :].astype(F32)
            out_ref[span, :half, :] = mine[:, :half] - (re * real - im * imag)
            out_ref[span, half:, :] = mine[:, half:] - (re * imag + im * real)
        rows = near_refs[0].shape[1]
        for shift in range(shifts):
            for part, near_ref in enumerate(near_refs):

                @pl.when((place_ref[1] == shift) & (step // span_of == part))
                def _():
                    out_ref[:, shift * rows : (shift + 1) * rows, :] += near_ref[...]


def downward(place, sigma, inc, interp_two, across, unfold, field, near_parts, shifts):
    grand, chunks, columns, lanes = inc.shape
    children, samples2, samples1 = interp_two.shape
    boxes, unknowns, _ = field.shape
    rows = near_parts[0].shape[1]
    parts = len(near_parts)
    pair = 2 if children % 2 == 0 else 1
    per = pair * (boxes // across.shape[0])
    each = boxes // per // parts
    return pl.pallas_call(
        functools.partial(down_kernel, children=children, pair=pair, parts=parts, shifts=shifts),
        grid=(grand * children,),
        out_shape=jax.ShapeDtypeStruct((boxes, unknowns, columns), F32),
        in_specs=[
            smem(),
            smem(),
            pl.BlockSpec((1, chunks, columns, lanes), lambda c: (c // children, 0, 0, 0)),
            pl.BlockSpec((1, samples2, samples1), lambda c: (c % children, 0, 0)),
            pl.BlockSpec((1, columns, samples1), lambda c: (c, 0, 0)),
            pl.BlockSpec(unfold.shape, lambda c: (0, 0)),
            pl.BlockSpec((per, unknowns, columns), lambda c: (c // pair, 0, 0)),
        ]
        + [
            pl.BlockSpec((per, rows, columns), lambda c, part=part: part_index(part, each)(c // pair))
            for part in range(parts)
        ],
        out_specs=pl.BlockSpec((per, unknowns, columns), lambda c: (c // pair, 0, 0)),
        scratch_shapes=[
            pltpu.VMEM((columns, chunks * lanes), BF16),
            pltpu.VMEM((pair * columns, samples1), BF16),
        ],
        compiler_params=params(56),
        cost_estimate=cost(6 * 10**9, 30 * 2**20),
        name="downward",
    )(place, sigma, inc, interp_two, across, unfold, field, *near_parts)


def join_kernel(place_ref, total_ref, *rest, parts):
    part_refs, out_ref = rest[:parts], rest[parts]
    each = pl.num_programs(0) // parts
    for part, part_ref in enumerate(part_refs):

        @pl.when(pl.program_id(0) // each == part)
        def _():
            out_ref[...] = total_ref[...] + part_ref[...].astype(F32)


def join(place, total, arrived):
    boxes, _, columns = total.shape
    count, rows, _ = arrived[0].shape
    parts = len(arrived)
    step = min(16, count)
    each = count // step
    half = pl.BlockSpec((step, rows, columns), lambda i, place_ref: (i, 1 - place_ref[1], 0))
    return pl.pallas_call(
        functools.partial(join_kernel, parts=parts),
        grid_spec=pltpu.PrefetchScalarGridSpec(
            num_scalar_prefetch=1,
            grid=(boxes // step,),
            in_specs=[half]
            + [
                pl.BlockSpec((step, rows, columns), lambda i, place_ref, part=part: part_index(part, each)(i))
                for part in range(parts)
            ],
            out_specs=half,
        ),
        out_shape=jax.ShapeDtypeStruct(total.shape, F32),
        input_output_aliases={1: 0},
        compiler_params=params(10),
        cost_estimate=cost(10**7, 5 * 2**20),
        name="join",
    )(place, total, *arrived)


def body(
    vectors, sigma, near_blocks, near_index, radiate, interp_one, interp_two, trans_one,
    level1_source, level1_offset, trans_two, level2_source, level2_offset,
):
    field = vectors[0]
    boxes, unknowns, columns = field.shape
    children, _, _ = interp_one.shape
    samples2 = interp_two.shape[1]
    parents = boxes // children
    grand = parents // children
    count = lax.axis_size("box")
    shifts = lax.axis_size("shift")
    place = jnp.stack([lax.axis_index("box"), lax.axis_index("shift")]).astype(jnp.int32)

    up = [(i, i + 1) for i in range(count - 1)]
    down = [(i + 1, i) for i in range(count - 1)]
    swap = [(s, shifts - 1 - s) for s in range(shifts)]
    pair_down = [(i + 1, i) for i in range(0, count - 1, 2)]
    odd_swap = [
        (i * shifts + s, i * shifts + shifts - 1 - s) for i in range(1, count, 2) for s in range(shifts)
    ]

    other = lax.ppermute(field, "shift", swap)
    high = lax.ppermute(field, "box", down)
    low = lax.ppermute(field, "box", up)

    folded, upper, turned = fold(
        interp_one, radiate, field.reshape(parents, children * unknowns, columns)
    )
    coarse = coarsen(interp_two, upper)
    chunk = samples2 // count
    pieces = coarse.reshape(grand, count, chunk, columns).swapaxes(0, 1)
    spread = lax.all_to_all(pieces, "box", split_axis=0, concat_axis=0, tiled=True)
    spread = spread.reshape(count * grand, chunk, columns)
    if chunk % 128 == 0:
        inc = level2(level2_offset, level2_source, trans_two, spread)
        inc = lax.all_to_all(
            inc.reshape(count, grand, columns, chunk), "box", split_axis=0, concat_axis=0, tiled=True
        ).swapaxes(0, 1)
    else:
        inc = weighted_lists(spread, trans_two, level2_offset, level2_source).astype(BF16)
        inc = lax.all_to_all(
            inc.reshape(count, grand, chunk, columns), "box", split_axis=0, concat_axis=0, tiled=True
        ).swapaxes(0, 1)
        inc = inc.reshape(grand, samples2 // 128, 128, columns).swapaxes(2, 3)

    relayed, other = lax.optimization_barrier((high, other))
    high_odd = lax.ppermute(relayed, ("box", "shift"), odd_swap)
    low_other = lax.ppermute(other, "box", up)
    high_even = lax.ppermute(other, "box", pair_down)

    wide = (parents, children * unknowns, columns)
    across, unfold = level1(
        place, level1_offset, level1_source, trans_one, folded, turned,
        low.reshape(wide), high.reshape(wide),
    )
    low, across = lax.optimization_barrier((low, across))
    splits = 2
    part = boxes // splits
    near_parts, arrived = [], []
    for one in range(splits):
        mine, theirs = near(
            place, near_index.T, near_blocks, low, field, high,
            low_other, other, high_even, high_odd, one * part, part,
        )
        near_parts.append(mine)
        arrived.append(lax.ppermute(theirs, "shift", swap))

    total = downward(place, sigma, inc, interp_two, across, unfold, field, near_parts, shifts)
    total = join(place, total, arrived)
    return total[None]


def solution(mesh):
    in_specs = (
        P("shift", "box", None, None),
        P("shift", None),
        P("box", None, "shift", None),
        P("box", None),
        P(),
        P(),
        P(),
        P(),
        P("box", None),
        P("box", None),
        P(None, "box"),
        P(),
        P(),
    )
    out_specs = P("shift", "box", None, None)

    return jax.shard_map(body, mesh=mesh, in_specs=in_specs, out_specs=out_specs, check_vma=False)
```

```python
import functools

import jax
import jax.numpy as jnp
from jax import lax
from jax.experimental import pallas as pl
from jax.experimental.pallas import tpu as pltpu
from jax.sharding import PartitionSpec as P


F32 = jnp.float32
BF16 = jnp.bfloat16
NT = (((1,), (1,)), ((), ()))


def vmem():
    return pl.BlockSpec(memory_space=pltpu.VMEM)


def smem():
    return pl.BlockSpec(memory_space=pltpu.SMEM)


def cost(flops, moved):
    return pl.CostEstimate(flops=flops, bytes_accessed=moved, transcendentals=0)


def params(mib):
    return pltpu.CompilerParams(vmem_limit_bytes=mib << 20)


def fold_kernel(one_ref, radiate_ref, field_ref, fold_ref, upper_ref, turned_ref):
    children, _, _ = one_ref.shape
    unknowns = radiate_ref.shape[1]
    pair, _, columns = field_ref.shape

    @pl.when(pl.program_id(0) == 0)
    def _():
        for child in range(children):
            fold_ref[:, child * unknowns : (child + 1) * unknowns] = jnp.dot(
                one_ref[child], radiate_ref[...], preferred_element_type=F32
            ).astype(BF16)

    wide = jnp.concatenate([field_ref[one] for one in range(pair)], axis=1)
    pattern = jnp.dot(fold_ref[...], wide, preferred_element_type=F32)
    for one in range(pair):
        mine = pattern[:, one * columns : (one + 1) * columns]
        upper_ref[one] = mine.astype(BF16)
        turned_ref[one] = mine.T.astype(BF16)


def fold(interp_one, radiate, field):
    children, samples1, _ = interp_one.shape
    unknowns = radiate.shape[1]
    parents, width, columns = field.shape
    pair = 2 if parents % 2 == 0 else 1
    return pl.pallas_call(
        fold_kernel,
        grid=(parents // pair,),
        out_shape=(
            jax.ShapeDtypeStruct((samples1, children * unknowns), BF16),
            jax.ShapeDtypeStruct((parents, samples1, columns), BF16),
            jax.ShapeDtypeStruct((parents, columns, samples1), BF16),
        ),
        in_specs=[
            pl.BlockSpec(interp_one.shape, lambda i: (0, 0, 0)),
            pl.BlockSpec(radiate.shape, lambda i: (0, 0)),
            pl.BlockSpec((pair, width, columns), lambda i: (i, 0, 0)),
        ],
        out_specs=(
            pl.BlockSpec((samples1, children * unknowns), lambda i: (0, 0)),
            pl.BlockSpec((pair, samples1, columns), lambda i: (i, 0, 0)),
            pl.BlockSpec((pair, columns, samples1), lambda i: (i, 0, 0)),
        ),
        compiler_params=params(56),
        cost_estimate=cost(3 * 10**9, 6 * 2**20),
        name="fold",
    )(interp_one, radiate, field)


def coarse_kernel(two_ref, upper_ref, out_ref):
    total = jnp.dot(two_ref[0], upper_ref[0], preferred_element_type=F32)
    for child in range(1, two_ref.shape[0]):
        total += jnp.dot(two_ref[child], upper_ref[child], preferred_element_type=F32)
    out_ref[0] = total.astype(BF16)


def coarsen(interp_two, upper):
    children, samples2, samples1 = interp_two.shape
    parents, _, columns = upper.shape
    grand = parents // children
    rows = min(samples2, 256)
    return pl.pallas_call(
        coarse_kernel,
        grid=(samples2 // rows, grand),
        out_shape=jax.ShapeDtypeStruct((grand, samples2, columns), BF16),
        in_specs=[
            pl.BlockSpec((children, rows, samples1), lambda q, g: (0, q, 0)),
            pl.BlockSpec((children, samples1, columns), lambda q, g: (g, 0, 0)),
        ],
        out_specs=pl.BlockSpec((1, rows, columns), lambda q, g: (g, q, 0)),
        compiler_params=params(56),
        cost_estimate=cost(4 * 10**9, 18 * 2**20),
        name="coarsen",
    )(interp_two, upper)


def live_count(source_ref, row):
    total = jnp.int32(0)
    for slot in range(source_ref.shape[1]):
        total += (source_ref[row, slot] >= 0).astype(jnp.int32)
    return total


def list_sum(offset_ref, source_ref, box, shape, weight_at, pattern_at, base):
    unroll = next(n for n in (4, 2, 1) if source_ref.shape[1] % n == 0)

    def add(trip, total):
        for one in range(unroll):
            slot = trip * unroll + one
            named = source_ref[box, slot]
            live = named >= 0
            weight = weight_at(offset_ref[box, slot]) * live.astype(F32)
            total = total + weight * pattern_at(jnp.where(live, named - base, 0))
        return total

    trips = (live_count(source_ref, box) + unroll - 1) // unroll
    return lax.fori_loop(0, trips, add, jnp.zeros(shape, F32))


def level2_kernel(offset_ref, source_ref, table_ref, pattern_ref, out_ref, turned_ref):
    boxes = pattern_ref.shape[0]

    def turn(box, carry):
        turned_ref[box] = pattern_ref[box].astype(F32).T
        return carry

    lax.fori_loop(0, boxes, turn, 0)

    def per_box(box, carry):
        total = list_sum(
            offset_ref, source_ref, box, turned_ref.shape[1:],
            lambda offset: table_ref[pl.ds(offset, 1), :], lambda source: turned_ref[source], 0,
        )
        out_ref[box] = total.astype(BF16)
        return carry

    lax.fori_loop(0, out_ref.shape[0], per_box, 0)


def level2(offset, source, table, pattern):
    boxes, samples, columns = pattern.shape
    return pl.pallas_call(
        level2_kernel,
        out_shape=jax.ShapeDtypeStruct((offset.shape[0], columns, samples), BF16),
        in_specs=[smem(), smem(), vmem(), vmem()],
        out_specs=vmem(),
        scratch_shapes=[pltpu.VMEM((boxes, columns, samples), F32)],
        compiler_params=params(8),
        cost_estimate=cost(3 * 10**9, 2 * 2**20),
        name="level2",
    )(offset, source, table, pattern)


def weighted_lists(pattern, table, offsets, sources):
    live = sources >= 0
    weights = table[offsets] * live[:, :, None].astype(F32)
    picked = pattern[jnp.where(live, sources, 0)]
    return jnp.einsum("cjk,cjkr->ckr", weights, picked, preferred_element_type=F32)


def level1_kernel(
    place_ref, offset_ref, source_ref, table_ref, fold_ref, turned_ref, low_ref, high_ref,
    across_ref, unfold_ref, rim_ref, rows_ref,
):
    step = pl.program_id(0)
    parents, columns, samples1 = turned_ref.shape
    width = rows_ref.shape[2]
    both = jnp.dot(
        fold_ref[...],
        jnp.concatenate([low_ref[0], high_ref[0]], axis=1),
        preferred_element_type=F32,
    )
    rim_ref[step] = both[:, :columns].T.astype(BF16).astype(F32)
    rim_ref[parents + step] = turned_ref[step].astype(F32)
    rim_ref[2 * parents + step] = both[:, columns:].T.astype(BF16).astype(F32)

    @pl.when(step == 0)
    def _():
        for part in range(rows_ref.shape[0]):
            rows_ref[part] = table_ref[:, part * width : (part + 1) * width]
        for first in range(0, fold_ref.shape[1], 128):
            unfold_ref[first : first + 128, :] = fold_ref[:, first : first + 128].T

    @pl.when(step == parents - 1)
    def _():
        def per_box(box, carry):
            for part in range(samples1 // width):
                lanes = slice(part * width, (part + 1) * width)
                across_ref[box, :, lanes] = list_sum(
                    offset_ref, source_ref, box, (columns, width),
                    lambda offset: rows_ref[part, pl.ds(offset, 1), :],
                    lambda source: rim_ref[source, :, lanes],
                    place_ref[0] * parents - parents,
                )
            return carry

        lax.fori_loop(0, parents, per_box, 0)


def level1(place, offset, source, table, folded, turned, low, high):
    parents, columns, samples1 = turned.shape
    around = pl.BlockSpec((1,) + low.shape[1:], lambda i: (i, 0, 0))
    return pl.pallas_call(
        level1_kernel,
        grid=(parents,),
        out_shape=(
            jax.ShapeDtypeStruct((parents, columns, samples1), F32),
            jax.ShapeDtypeStruct((folded.shape[1], folded.shape[0]), BF16),
        ),
        in_specs=[smem()] * 3
        + [
            pl.BlockSpec(table.shape, lambda i: (0, 0)),
            pl.BlockSpec(folded.shape, lambda i: (0, 0)),
            pl.BlockSpec(turned.shape, lambda i: (0, 0, 0)),
            around,
            around,
        ],
        out_specs=(
            pl.BlockSpec((parents, columns, samples1), lambda i: (0, 0, 0)),
            pl.BlockSpec((folded.shape[1], folded.shape[0]), lambda i: (0, 0)),
        ),
        scratch_shapes=[
            pltpu.VMEM((3 * parents, columns, samples1), F32),
            pltpu.VMEM((samples1 // 128, table.shape[0], 128), F32),
        ],
        compiler_params=params(56),
        cost_estimate=cost(8 * 10**9, 14 * 2**20),
        name="level1",
    )(place, offset, source, table, folded, turned, low, high)


def near_kernel(
    place_ref, index_ref, blocks_ref, low_ref, own_ref, high_ref, odd_ref, *rest, first, count, cuts,
):
    swapped_refs, piece_refs, even_refs = rest[: cuts[0]], rest[cuts[0] : cuts[1]], rest[cuts[1] : -4]
    mine_ref, theirs_ref, field_ref, sem = rest[-4:]
    step = pl.program_id(0)
    place = place_ref[0]
    boxes, _, columns = own_ref.shape
    chunk, slots = blocks_ref.shape[:2]

    def into(ref, source, length, target, side, lane):
        return pltpu.make_async_copy(
            ref.at[pl.ds(source, length)],
            field_ref.at[pl.ds(target, length), :, pl.ds(side * columns, columns)],
            sem.at[lane],
        )

    copies = [
        into(low_ref, first, boxes - first, first, 0, 0),
        into(own_ref, 0, boxes, boxes, 0, 1),
        into(high_ref, 0, first + count, 2 * boxes, 0, 2),
    ]
    lane = 3
    for refs, target in ((swapped_refs, boxes), (piece_refs, first)):
        for one, ref in enumerate(refs):
            length = ref.shape[0]
            copies.append(into(ref, 0, length, target + one * length, 1, lane))
            lane += 1
    even = []
    for one, ref in enumerate(even_refs):
        length = ref.shape[0]
        even.append(into(ref, 0, length, 2 * boxes + one * length, 1, lane))
        lane += 1
    odd = into(odd_ref, 0, first + count, 2 * boxes, 1, lane)

    @pl.when(step == 0)
    def _():
        for copy in copies:
            copy.start()

        @pl.when(place % 2 == 0)
        def _():
            for copy in even:
                copy.start()
            for copy in even:
                copy.wait()

        @pl.when(place % 2 == 1)
        def _():
            odd.start()
            odd.wait()

        for copy in copies:
            copy.wait()

    base = place * boxes - boxes
    for box in range(chunk):
        row = first + step * chunk + box
        total = None
        for slot in range(0, slots, 2):
            left, right = [], []
            for one in range(slot, min(slot + 2, slots)):
                block = blocks_ref[box, one]
                if one == 0:
                    where = boxes + row
                else:
                    named = index_ref[one, row]
                    live = named >= 0
                    where = jnp.where(live, named - base, boxes)
                    block = jnp.where(live, block, jnp.zeros_like(block))
                left.append(block)
                right.append(field_ref[where])
            part = jnp.dot(
                jnp.concatenate(left, axis=1),
                jnp.concatenate(right, axis=0),
                preferred_element_type=F32,
            )
            total = part if total is None else total + part
        mine_ref[box] = total[:, :columns]
        theirs_ref[box] = total[:, columns:].astype(BF16)


def near(place, index, blocks, low, own, high, odd, swapped, pieces, evens, first, count):
    boxes, unknowns, columns = own.shape
    _, slots, rows, _ = blocks.shape
    chunk = min(8, count)
    lanes = len(swapped) + len(pieces) + len(evens)
    hbm = pl.BlockSpec(memory_space=pl.ANY)
    return pl.pallas_call(
        functools.partial(
            near_kernel, first=first, count=count,
            cuts=(len(swapped), len(swapped) + len(pieces)),
        ),
        grid=(count // chunk,),
        out_shape=(
            jax.ShapeDtypeStruct((count, rows, columns), F32),
            jax.ShapeDtypeStruct((count, rows, columns), BF16),
        ),
        in_specs=[
            smem(),
            smem(),
            pl.BlockSpec((chunk, slots, rows, unknowns), lambda i: (first // chunk + i, 0, 0, 0)),
        ]
        + [hbm] * (4 + lanes),
        out_specs=(pl.BlockSpec((chunk, rows, columns), lambda i: (i, 0, 0)),) * 2,
        scratch_shapes=[
            pltpu.VMEM((3 * boxes, unknowns, 2 * columns), BF16),
            pltpu.SemaphoreType.DMA((4 + lanes,)),
        ],
        compiler_params=params(56),
        cost_estimate=cost(count * 2 * 10**8, 14 * 2**20 + count * 10**5),
    )(place, index, blocks, low, own, high, odd, *swapped, *pieces, *evens)


def part_index(which, per):
    return lambda i: (jnp.clip(i - which * per, 0, per - 1), 0, 0)


def down_kernel(place_ref, sigma_ref, inc_ref, two_ref, across_ref, unfold_ref, field_ref, *rest, children, pair, parts, shifts):
    near_refs, (out_ref, flat_ref, local_ref) = rest[:parts], rest[parts:]
    chunks, columns, lanes = inc_ref.shape[1:]
    step = pl.program_id(0)
    span_of = pl.num_programs(0) // parts

    @pl.when(step % children == 0)
    def _():
        for one in range(chunks):
            flat_ref[:, one * lanes : (one + 1) * lanes] = inc_ref[0, one]

    down = jnp.dot(flat_ref[...], two_ref[0], preferred_element_type=F32)
    local_ref[pl.ds((step % pair) * columns, columns), :] = (down + across_ref[0]).astype(BF16)

    @pl.when(step % pair == pair - 1)
    def _():
        far = lax.dot_general(unfold_ref[...], local_ref[...], NT, preferred_element_type=F32)
        boxes, unknowns, _ = out_ref.shape
        per = boxes // pair
        half = unknowns // 2
        re, im = sigma_ref[0, 0], sigma_ref[0, 1]
        for one in range(pair):
            mine = far[:, one * columns : (one + 1) * columns].reshape(per, unknowns, columns)
            span = slice(one * per, (one + 1) * per)
            real = field_ref[span, :half, :].astype(F32)
            imag = field_ref[span, half:, :].astype(F32)
            out_ref[span, :half, :] = mine[:, :half] - (re * real - im * imag)
            out_ref[span, half:, :] = mine[:, half:] - (re * imag + im * real)
        rows = near_refs[0].shape[1]
        for shift in range(shifts):
            for part, near_ref in enumerate(near_refs):

                @pl.when((place_ref[1] == shift) & (step // span_of == part))
                def _():
                    out_ref[:, shift * rows : (shift + 1) * rows, :] += near_ref[...]


def downward(place, sigma, inc, interp_two, across, unfold, field, near_parts, shifts):
    grand, chunks, columns, lanes = inc.shape
    children, samples2, samples1 = interp_two.shape
    boxes, unknowns, _ = field.shape
    rows = near_parts[0].shape[1]
    parts = len(near_parts)
    pair = 2 if children % 2 == 0 else 1
    per = pair * (boxes // across.shape[0])
    each = boxes // per // parts
    return pl.pallas_call(
        functools.partial(down_kernel, children=children, pair=pair, parts=parts, shifts=shifts),
        grid=(grand * children,),
        out_shape=jax.ShapeDtypeStruct((boxes, unknowns, columns), F32),
        in_specs=[
            smem(),
            smem(),
            pl.BlockSpec((1, chunks, columns, lanes), lambda c: (c // children, 0, 0, 0)),
            pl.BlockSpec((1, samples2, samples1), lambda c: (c % children, 0, 0)),
            pl.BlockSpec((1, columns, samples1), lambda c: (c, 0, 0)),
            pl.BlockSpec(unfold.shape, lambda c: (0, 0)),
            pl.BlockSpec((per, unknowns, columns), lambda c: (c // pair, 0, 0)),
        ]
        + [
            pl.BlockSpec((per, rows, columns), lambda c, part=part: part_index(part, each)(c // pair))
            for part in range(parts)
        ],
        out_specs=pl.BlockSpec((per, unknowns, columns), lambda c: (c // pair, 0, 0)),
        scratch_shapes=[
            pltpu.VMEM((columns, chunks * lanes), BF16),
            pltpu.VMEM((pair * columns, samples1), BF16),
        ],
        compiler_params=params(56),
        cost_estimate=cost(6 * 10**9, 30 * 2**20),
        name="downward",
    )(place, sigma, inc, interp_two, across, unfold, field, *near_parts)


def join_kernel(place_ref, total_ref, *rest, parts):
    part_refs, out_ref = rest[:parts], rest[parts]
    each = pl.num_programs(0) // parts
    for part, part_ref in enumerate(part_refs):

        @pl.when(pl.program_id(0) // each == part)
        def _():
            out_ref[...] = total_ref[...] + part_ref[...].astype(F32)


def join(place, total, arrived):
    boxes, _, columns = total.shape
    count, rows, _ = arrived[0].shape
    parts = len(arrived)
    step = min(16, count)
    each = count // step
    half = pl.BlockSpec((step, rows, columns), lambda i, place_ref: (i, 1 - place_ref[1], 0))
    return pl.pallas_call(
        functools.partial(join_kernel, parts=parts),
        grid_spec=pltpu.PrefetchScalarGridSpec(
            num_scalar_prefetch=1,
            grid=(boxes // step,),
            in_specs=[half]
            + [
                pl.BlockSpec((step, rows, columns), lambda i, place_ref, part=part: part_index(part, each)(i))
                for part in range(parts)
            ],
            out_specs=half,
        ),
        out_shape=jax.ShapeDtypeStruct(total.shape, F32),
        input_output_aliases={1: 0},
        compiler_params=params(10),
        cost_estimate=cost(10**7, 5 * 2**20),
        name="join",
    )(place, total, *arrived)


def body(
    vectors, sigma, near_blocks, near_index, radiate, interp_one, interp_two, trans_one,
    level1_source, level1_offset, trans_two, level2_source, level2_offset,
):
    field = vectors[0]
    boxes, unknowns, columns = field.shape
    children, _, _ = interp_one.shape
    samples2 = interp_two.shape[1]
    parents = boxes // children
    grand = parents // children
    count = lax.axis_size("box")
    shifts = lax.axis_size("shift")
    place = jnp.stack([lax.axis_index("box"), lax.axis_index("shift")]).astype(jnp.int32)

    up = [(i, i + 1) for i in range(count - 1)]
    down = [(i + 1, i) for i in range(count - 1)]
    swap = [(s, shifts - 1 - s) for s in range(shifts)]
    pair_down = [(i + 1, i) for i in range(0, count - 1, 2)]
    odd_swap = [
        (i * shifts + s, i * shifts + shifts - 1 - s) for i in range(1, count, 2) for s in range(shifts)
    ]

    splits = 2
    part = boxes // splits
    swapped = [None] * splits
    for one in reversed(range(splits)):
        swapped[one] = lax.ppermute(
            lax.slice_in_dim(field, one * part, (one + 1) * part, axis=0), "shift", swap
        )
    high = lax.ppermute(field, "box", down)
    low = lax.ppermute(field, "box", up)

    folded, upper, turned = fold(
        interp_one, radiate, field.reshape(parents, children * unknowns, columns)
    )
    coarse = coarsen(interp_two, upper)
    chunk = samples2 // count
    pieces = coarse.reshape(grand, count, chunk, columns).swapaxes(0, 1)
    spread = lax.all_to_all(pieces, "box", split_axis=0, concat_axis=0, tiled=True)
    spread = spread.reshape(count * grand, chunk, columns)
    if chunk % 128 == 0:
        inc = level2(level2_offset, level2_source, trans_two, spread)
        inc = lax.all_to_all(
            inc.reshape(count, grand, columns, chunk), "box", split_axis=0, concat_axis=0, tiled=True
        )
        inc = inc.swapaxes(0, 1)
    else:
        inc = weighted_lists(spread, trans_two, level2_offset, level2_source).astype(BF16)
        inc = lax.all_to_all(
            inc.reshape(count, grand, chunk, columns), "box", split_axis=0, concat_axis=0, tiled=True
        )
        inc = inc.swapaxes(0, 1)
        inc = inc.reshape(grand, samples2 // 128, 128, columns).swapaxes(2, 3)

    pieces, evens = [], []
    for one in range(splits):
        pieces.append(lax.ppermute(swapped[one], "box", up))
    for one in range(splits):
        evens.append(lax.ppermute(swapped[one], "box", pair_down))
    high_odd = lax.ppermute(high, ("box", "shift"), odd_swap)

    wide = (parents, children * unknowns, columns)
    across, unfold = level1(
        place, level1_offset, level1_source, trans_one, folded, turned,
        low.reshape(wide), high.reshape(wide),
    )
    low, across = lax.optimization_barrier((low, across))
    near_parts, arrived = [None] * splits, [None] * splits
    for one in reversed(range(splits)):
        mine, theirs = near(
            place, near_index.T, near_blocks, low, field, high, high_odd,
            swapped, pieces[one:], evens[: one + 1], one * part, part,
        )
        near_parts[one] = mine
        arrived[one] = lax.ppermute(theirs, "shift", swap)

    total = downward(place, sigma, inc, interp_two, across, unfold, field, near_parts, shifts)
    total = join(place, total, arrived)
    return total[None]


def solution(mesh):
    in_specs = (
        P("shift", "box", None, None),
        P("shift", None),
        P("box", None, "shift", None),
        P("box", None),
        P(),
        P(),
        P(),
        P(),
        P("box", None),
        P("box", None),
        P(None, "box"),
        P(),
        P(),
    )
    out_specs = P("shift", "box", None, None)

    return jax.shard_map(body, mesh=mesh, in_specs=in_specs, out_specs=out_specs, check_vma=False)
```

```python
import functools

import jax
import jax.numpy as jnp
from jax import lax
from jax.experimental import pallas as pl
from jax.experimental.pallas import tpu as pltpu
from jax.sharding import PartitionSpec as P


F32 = jnp.float32
BF16 = jnp.bfloat16
NT = (((1,), (1,)), ((), ()))


def vmem():
    return pl.BlockSpec(memory_space=pltpu.VMEM)


def smem():
    return pl.BlockSpec(memory_space=pltpu.SMEM)


def cost(flops, moved):
    return pl.CostEstimate(flops=flops, bytes_accessed=moved, transcendentals=0)


def params(mib):
    return pltpu.CompilerParams(vmem_limit_bytes=mib << 20)


def fold_kernel(one_ref, radiate_ref, field_ref, fold_ref, upper_ref, turned_ref):
    children, _, _ = one_ref.shape
    unknowns = radiate_ref.shape[1]
    pair, _, columns = field_ref.shape

    @pl.when(pl.program_id(0) == 0)
    def _():
        for child in range(children):
            fold_ref[:, child * unknowns : (child + 1) * unknowns] = jnp.dot(
                one_ref[child], radiate_ref[...], preferred_element_type=F32
            ).astype(BF16)

    wide = jnp.concatenate([field_ref[one] for one in range(pair)], axis=1)
    pattern = jnp.dot(fold_ref[...], wide, preferred_element_type=F32)
    for one in range(pair):
        mine = pattern[:, one * columns : (one + 1) * columns]
        upper_ref[one] = mine.astype(BF16)
        turned_ref[one] = mine.T.astype(BF16)


def fold(interp_one, radiate, field):
    children, samples1, _ = interp_one.shape
    unknowns = radiate.shape[1]
    parents, width, columns = field.shape
    pair = 2 if parents % 2 == 0 else 1
    return pl.pallas_call(
        fold_kernel,
        grid=(parents // pair,),
        out_shape=(
            jax.ShapeDtypeStruct((samples1, children * unknowns), BF16),
            jax.ShapeDtypeStruct((parents, samples1, columns), BF16),
            jax.ShapeDtypeStruct((parents, columns, samples1), BF16),
        ),
        in_specs=[
            pl.BlockSpec(interp_one.shape, lambda i: (0, 0, 0)),
            pl.BlockSpec(radiate.shape, lambda i: (0, 0)),
            pl.BlockSpec((pair, width, columns), lambda i: (i, 0, 0)),
        ],
        out_specs=(
            pl.BlockSpec((samples1, children * unknowns), lambda i: (0, 0)),
            pl.BlockSpec((pair, samples1, columns), lambda i: (i, 0, 0)),
            pl.BlockSpec((pair, columns, samples1), lambda i: (i, 0, 0)),
        ),
        compiler_params=params(56),
        cost_estimate=cost(3 * 10**9, 6 * 2**20),
        name="fold",
    )(interp_one, radiate, field)


def coarse_kernel(two_ref, upper_ref, out_ref):
    total = jnp.dot(two_ref[0], upper_ref[0], preferred_element_type=F32)
    for child in range(1, two_ref.shape[0]):
        total += jnp.dot(two_ref[child], upper_ref[child], preferred_element_type=F32)
    out_ref[0] = total.astype(BF16)


def coarsen(interp_two, upper):
    children, samples2, samples1 = interp_two.shape
    parents, _, columns = upper.shape
    grand = parents // children
    rows = min(samples2, 256)
    return pl.pallas_call(
        coarse_kernel,
        grid=(samples2 // rows, grand),
        out_shape=jax.ShapeDtypeStruct((grand, samples2, columns), BF16),
        in_specs=[
            pl.BlockSpec((children, rows, samples1), lambda q, g: (0, q, 0)),
            pl.BlockSpec((children, samples1, columns), lambda q, g: (g, 0, 0)),
        ],
        out_specs=pl.BlockSpec((1, rows, columns), lambda q, g: (g, q, 0)),
        compiler_params=params(56),
        cost_estimate=cost(4 * 10**9, 18 * 2**20),
        name="coarsen",
    )(interp_two, upper)


def live_count(source_ref, row):
    total = jnp.int32(0)
    for slot in range(source_ref.shape[1]):
        total += (source_ref[row, slot] >= 0).astype(jnp.int32)
    return total


def list_sum(offset_ref, source_ref, box, count, shape, weight_at, pattern_at, base):
    unroll = next(n for n in (4, 2, 1) if source_ref.shape[1] % n == 0)

    def add(trip, total):
        for one in range(unroll):
            slot = trip * unroll + one
            named = source_ref[box, slot]
            live = named >= 0
            weight = weight_at(offset_ref[box, slot]) * live.astype(F32)
            total = total + weight * pattern_at(jnp.where(live, named - base, 0))
        return total

    trips = (count + unroll - 1) // unroll
    return lax.fori_loop(0, trips, add, jnp.zeros(shape, F32))


def level2_kernel(offset_ref, source_ref, table_ref, pattern_ref, out_ref, turned_ref):
    boxes = pattern_ref.shape[0]

    def turn(box, carry):
        turned_ref[box] = pattern_ref[box].astype(F32).T
        return carry

    lax.fori_loop(0, boxes, turn, 0)

    def per_box(box, carry):
        total = list_sum(
            offset_ref, source_ref, box, live_count(source_ref, box), turned_ref.shape[1:],
            lambda offset: table_ref[pl.ds(offset, 1), :], lambda source: turned_ref[source], 0,
        )
        out_ref[box] = total.astype(BF16)
        return carry

    lax.fori_loop(0, out_ref.shape[0], per_box, 0)


def level2(offset, source, table, pattern):
    boxes, samples, columns = pattern.shape
    return pl.pallas_call(
        level2_kernel,
        out_shape=jax.ShapeDtypeStruct((offset.shape[0], columns, samples), BF16),
        in_specs=[smem(), smem(), vmem(), vmem()],
        out_specs=vmem(),
        scratch_shapes=[pltpu.VMEM((boxes, columns, samples), F32)],
        compiler_params=params(8),
        cost_estimate=cost(3 * 10**9, 2 * 2**20),
        name="level2",
    )(offset, source, table, pattern)


def weighted_lists(pattern, table, offsets, sources):
    live = sources >= 0
    weights = table[offsets] * live[:, :, None].astype(F32)
    picked = pattern[jnp.where(live, sources, 0)]
    return jnp.einsum("cjk,cjkr->ckr", weights, picked, preferred_element_type=F32)


def rise_kernel(fold_ref, turned_ref, high_ref, around_ref, unfold_ref):
    pair, _, columns = high_ref.shape

    @pl.when(pl.program_id(0) == 0)
    def _():
        for first in range(0, fold_ref.shape[1], 128):
            unfold_ref[first : first + 128, :] = fold_ref[:, first : first + 128].T

    wide = jnp.concatenate([high_ref[one] for one in range(pair)], axis=1)
    pattern = jnp.dot(fold_ref[...], wide, preferred_element_type=F32)
    for one in range(pair):
        around_ref[0, one] = turned_ref[one].astype(F32)
        around_ref[1, one] = pattern[:, one * columns : (one + 1) * columns].T.astype(BF16).astype(F32)


def rise(folded, turned, high):
    parents, columns, samples1 = turned.shape
    width = high.shape[1]
    pair = 2 if parents % 2 == 0 else 1
    return pl.pallas_call(
        rise_kernel,
        grid=(parents // pair,),
        out_shape=(
            jax.ShapeDtypeStruct((2, parents, columns, samples1), F32),
            jax.ShapeDtypeStruct((folded.shape[1], folded.shape[0]), BF16),
        ),
        in_specs=[
            pl.BlockSpec(folded.shape, lambda i: (0, 0)),
            pl.BlockSpec((pair, columns, samples1), lambda i: (i, 0, 0)),
            pl.BlockSpec((pair, width, columns), lambda i: (i, 0, 0)),
        ],
        out_specs=(
            pl.BlockSpec((2, pair, columns, samples1), lambda i: (0, i, 0, 0)),
            pl.BlockSpec((folded.shape[1], folded.shape[0]), lambda i: (0, 0)),
        ),
        compiler_params=params(56),
        cost_estimate=cost(2 * 10**9, 10 * 2**20),
        name="rise",
    )(folded, turned, high)


def level1_kernel(
    place_ref, offset_ref, source_ref, table_ref, fold_ref, low_ref, around_ref,
    across_ref, rim_ref, rows_ref, sem,
):
    step = pl.program_id(0)
    pair, _, columns = low_ref.shape
    parents, _, samples1 = across_ref.shape
    width = rows_ref.shape[2]

    def around(which):
        return pltpu.make_async_copy(
            around_ref.at[which], rim_ref.at[pl.ds((which + 1) * parents, parents)], sem.at[which]
        )

    @pl.when(step == 0)
    def _():
        around(0).start()
        around(1).start()
        for part in range(rows_ref.shape[0]):
            rows_ref[part] = table_ref[:, part * width : (part + 1) * width]

    wide = jnp.concatenate([low_ref[one] for one in range(pair)], axis=1)
    pattern = jnp.dot(fold_ref[...], wide, preferred_element_type=F32)
    for one in range(pair):
        rim_ref[step * pair + one] = (
            pattern[:, one * columns : (one + 1) * columns].T.astype(BF16).astype(F32)
        )

    @pl.when(step == pl.num_programs(0) - 1)
    def _():
        around(0).wait()
        around(1).wait()

        def per_box(box, carry):
            count = live_count(source_ref, box)
            for part in range(samples1 // width):
                lanes = slice(part * width, (part + 1) * width)
                across_ref[box, :, lanes] = list_sum(
                    offset_ref, source_ref, box, count, (columns, width),
                    lambda offset: rows_ref[part, pl.ds(offset, 1), :],
                    lambda source: rim_ref[source, :, lanes],
                    place_ref[0] * parents - parents,
                )
            return carry

        lax.fori_loop(0, parents, per_box, 0)


def level1(place, offset, source, table, folded, low, around):
    _, parents, columns, samples1 = around.shape
    pair = 2 if parents % 2 == 0 else 1
    return pl.pallas_call(
        level1_kernel,
        grid=(parents // pair,),
        out_shape=jax.ShapeDtypeStruct((parents, columns, samples1), F32),
        in_specs=[smem()] * 3
        + [
            pl.BlockSpec(table.shape, lambda i: (0, 0)),
            pl.BlockSpec(folded.shape, lambda i: (0, 0)),
            pl.BlockSpec((pair,) + low.shape[1:], lambda i: (i, 0, 0)),
            pl.BlockSpec(memory_space=pl.ANY),
        ],
        out_specs=pl.BlockSpec((parents, columns, samples1), lambda i: (0, 0, 0)),
        scratch_shapes=[
            pltpu.VMEM((3 * parents, columns, samples1), F32),
            pltpu.VMEM((samples1 // 128, table.shape[0], 128), F32),
            pltpu.SemaphoreType.DMA((2,)),
        ],
        compiler_params=params(56),
        cost_estimate=cost(6 * 10**9, 12 * 2**20),
        name="level1",
    )(place, offset, source, table, folded, low, around)


def near_kernel(
    place_ref, index_ref, blocks_ref, low_ref, own_ref, high_ref, odd_ref, *rest, first, count, cuts,
):
    swapped_refs, piece_refs, even_refs = rest[: cuts[0]], rest[cuts[0] : cuts[1]], rest[cuts[1] : -4]
    mine_ref, theirs_ref, field_ref, sem = rest[-4:]
    step = pl.program_id(0)
    place = place_ref[0]
    boxes, _, columns = own_ref.shape
    chunk, slots = blocks_ref.shape[:2]

    def into(ref, source, length, target, side, lane):
        return pltpu.make_async_copy(
            ref.at[pl.ds(source, length)],
            field_ref.at[pl.ds(target, length), :, pl.ds(side * columns, columns)],
            sem.at[lane],
        )

    copies = [
        into(low_ref, first, boxes - first, first, 0, 0),
        into(own_ref, 0, boxes, boxes, 0, 1),
        into(high_ref, 0, first + count, 2 * boxes, 0, 2),
    ]
    lane = 3
    for refs, target in ((swapped_refs, boxes), (piece_refs, first)):
        for one, ref in enumerate(refs):
            length = ref.shape[0]
            copies.append(into(ref, 0, length, target + one * length, 1, lane))
            lane += 1
    even = []
    for one, ref in enumerate(even_refs):
        length = ref.shape[0]
        even.append(into(ref, 0, length, 2 * boxes + one * length, 1, lane))
        lane += 1
    odd = into(odd_ref, 0, first + count, 2 * boxes, 1, lane)

    @pl.when(step == 0)
    def _():
        for copy in copies:
            copy.start()

        @pl.when(place % 2 == 0)
        def _():
            for copy in even:
                copy.start()
            for copy in even:
                copy.wait()

        @pl.when(place % 2 == 1)
        def _():
            odd.start()
            odd.wait()

        for copy in copies:
            copy.wait()

    base = place * boxes - boxes
    for box in range(chunk):
        row = first + step * chunk + box
        total = None
        for slot in range(0, slots, 2):
            left, right = [], []
            for one in range(slot, min(slot + 2, slots)):
                block = blocks_ref[box, one]
                if one == 0:
                    where = boxes + row
                else:
                    named = index_ref[one, row]
                    live = named >= 0
                    where = jnp.where(live, named - base, boxes)
                    block = jnp.where(live, block, jnp.zeros_like(block))
                left.append(block)
                right.append(field_ref[where])
            part = jnp.dot(
                jnp.concatenate(left, axis=1),
                jnp.concatenate(right, axis=0),
                preferred_element_type=F32,
            )
            total = part if total is None else total + part
        mine_ref[box] = total[:, :columns]
        theirs_ref[box] = total[:, columns:].astype(BF16)


def near(place, index, blocks, low, own, high, odd, swapped, pieces, evens, first, count):
    boxes, unknowns, columns = own.shape
    _, slots, rows, _ = blocks.shape
    chunk = min(8, count)
    lanes = len(swapped) + len(pieces) + len(evens)
    hbm = pl.BlockSpec(memory_space=pl.ANY)
    return pl.pallas_call(
        functools.partial(
            near_kernel, first=first, count=count,
            cuts=(len(swapped), len(swapped) + len(pieces)),
        ),
        grid=(count // chunk,),
        out_shape=(
            jax.ShapeDtypeStruct((count, rows, columns), F32),
            jax.ShapeDtypeStruct((count, rows, columns), BF16),
        ),
        in_specs=[
            smem(),
            smem(),
            pl.BlockSpec((chunk, slots, rows, unknowns), lambda i: (first // chunk + i, 0, 0, 0)),
        ]
        + [hbm] * (4 + lanes),
        out_specs=(pl.BlockSpec((chunk, rows, columns), lambda i: (i, 0, 0)),) * 2,
        scratch_shapes=[
            pltpu.VMEM((3 * boxes, unknowns, 2 * columns), BF16),
            pltpu.SemaphoreType.DMA((4 + lanes,)),
        ],
        compiler_params=params(56),
        cost_estimate=cost(count * 2 * 10**8, 14 * 2**20 + count * 10**5),
    )(place, index, blocks, low, own, high, odd, *swapped, *pieces, *evens)


def part_index(which, per):
    return lambda i: (jnp.clip(i - which * per, 0, per - 1), 0, 0)


def down_kernel(place_ref, sigma_ref, inc_ref, two_ref, across_ref, unfold_ref, field_ref, *rest, children, pair, parts, shifts):
    near_refs, early_ref, (out_ref, flat_ref, local_ref) = rest[:parts], rest[parts], rest[parts + 1 :]
    chunks, columns, lanes = inc_ref.shape[1:]
    step = pl.program_id(0)
    span_of = pl.num_programs(0) // parts

    @pl.when(step % children == 0)
    def _():
        for one in range(chunks):
            flat_ref[:, one * lanes : (one + 1) * lanes] = inc_ref[0, one]

    down = jnp.dot(flat_ref[...], two_ref[0], preferred_element_type=F32)
    local_ref[pl.ds((step % pair) * columns, columns), :] = (down + across_ref[0]).astype(BF16)

    @pl.when(step % pair == pair - 1)
    def _():
        far = lax.dot_general(unfold_ref[...], local_ref[...], NT, preferred_element_type=F32)
        boxes, unknowns, _ = out_ref.shape
        per = boxes // pair
        half = unknowns // 2
        re, im = sigma_ref[0, 0], sigma_ref[0, 1]
        for one in range(pair):
            mine = far[:, one * columns : (one + 1) * columns].reshape(per, unknowns, columns)
            span = slice(one * per, (one + 1) * per)
            real = field_ref[span, :half, :].astype(F32)
            imag = field_ref[span, half:, :].astype(F32)
            out_ref[span, :half, :] = mine[:, :half] - (re * real - im * imag)
            out_ref[span, half:, :] = mine[:, half:] - (re * imag + im * real)
        rows = near_refs[0].shape[1]
        for shift in range(shifts):
            for part, near_ref in enumerate(near_refs):

                @pl.when((place_ref[1] == shift) & (step // span_of == part))
                def _():
                    out_ref[:, shift * rows : (shift + 1) * rows, :] += near_ref[...]

            @pl.when((place_ref[1] == shift) & (step // span_of == parts - 1))
            def _():
                there = shifts - 1 - shift
                out_ref[:, there * rows : (there + 1) * rows, :] += early_ref[...].astype(F32)


def downward(place, sigma, inc, interp_two, across, unfold, field, near_parts, early, shifts):
    grand, chunks, columns, lanes = inc.shape
    children, samples2, samples1 = interp_two.shape
    boxes, unknowns, _ = field.shape
    rows = near_parts[0].shape[1]
    parts = len(near_parts)
    pair = 2 if children % 2 == 0 else 1
    per = pair * (boxes // across.shape[0])
    each = boxes // per // parts
    return pl.pallas_call(
        functools.partial(down_kernel, children=children, pair=pair, parts=parts, shifts=shifts),
        grid=(grand * children,),
        out_shape=jax.ShapeDtypeStruct((boxes, unknowns, columns), F32),
        in_specs=[
            smem(),
            smem(),
            pl.BlockSpec((1, chunks, columns, lanes), lambda c: (c // children, 0, 0, 0)),
            pl.BlockSpec((1, samples2, samples1), lambda c: (c % children, 0, 0)),
            pl.BlockSpec((1, columns, samples1), lambda c: (c, 0, 0)),
            pl.BlockSpec(unfold.shape, lambda c: (0, 0)),
            pl.BlockSpec((per, unknowns, columns), lambda c: (c // pair, 0, 0)),
        ]
        + [
            pl.BlockSpec((per, rows, columns), lambda c, part=part: part_index(part, each)(c // pair))
            for part in list(range(parts)) + [parts - 1]
        ],
        out_specs=pl.BlockSpec((per, unknowns, columns), lambda c: (c // pair, 0, 0)),
        scratch_shapes=[
            pltpu.VMEM((columns, chunks * lanes), BF16),
            pltpu.VMEM((pair * columns, samples1), BF16),
        ],
        compiler_params=params(56),
        cost_estimate=cost(6 * 10**9, 30 * 2**20),
        name="downward",
    )(place, sigma, inc, interp_two, across, unfold, field, *near_parts, early)


def join_kernel(place_ref, total_ref, part_ref, out_ref):
    out_ref[...] = total_ref[...] + part_ref[...].astype(F32)


def join(place, total, part):
    count, rows, columns = part.shape
    step = min(16, count)
    half = pl.BlockSpec((step, rows, columns), lambda i, place_ref: (i, 1 - place_ref[1], 0))
    return pl.pallas_call(
        join_kernel,
        grid_spec=pltpu.PrefetchScalarGridSpec(
            num_scalar_prefetch=1,
            grid=(count // step,),
            in_specs=[half, pl.BlockSpec((step, rows, columns), lambda i, place_ref: (i, 0, 0))],
            out_specs=half,
        ),
        out_shape=jax.ShapeDtypeStruct(total.shape, F32),
        input_output_aliases={1: 0},
        compiler_params=params(10),
        cost_estimate=cost(10**7, 3 * 2**20),
        name="join",
    )(place, total, part)


def body(
    vectors, sigma, near_blocks, near_index, radiate, interp_one, interp_two, trans_one,
    level1_source, level1_offset, trans_two, level2_source, level2_offset,
):
    field = vectors[0]
    boxes, unknowns, columns = field.shape
    children, _, _ = interp_one.shape
    samples2 = interp_two.shape[1]
    parents = boxes // children
    grand = parents // children
    count = lax.axis_size("box")
    shifts = lax.axis_size("shift")
    place = jnp.stack([lax.axis_index("box"), lax.axis_index("shift")]).astype(jnp.int32)

    up = [(i, i + 1) for i in range(count - 1)]
    down = [(i + 1, i) for i in range(count - 1)]
    swap = [(s, shifts - 1 - s) for s in range(shifts)]
    pair_down = [(i + 1, i) for i in range(0, count - 1, 2)]
    odd_swap = [
        (i * shifts + s, i * shifts + shifts - 1 - s) for i in range(1, count, 2) for s in range(shifts)
    ]

    splits = 2
    part = boxes // splits
    swapped = [None] * splits
    for one in reversed(range(splits)):
        swapped[one] = lax.ppermute(
            lax.slice_in_dim(field, one * part, (one + 1) * part, axis=0), "shift", swap
        )
    high = lax.ppermute(field, "box", down)
    low = lax.ppermute(field, "box", up)

    folded, upper, turned = fold(
        interp_one, radiate, field.reshape(parents, children * unknowns, columns)
    )
    coarse = coarsen(interp_two, upper)
    chunk = samples2 // count
    pieces = coarse.reshape(grand, count, chunk, columns).swapaxes(0, 1)
    spread = lax.all_to_all(pieces, "box", split_axis=0, concat_axis=0, tiled=True)
    spread = spread.reshape(count * grand, chunk, columns)
    if chunk % 128 == 0:
        inc = level2(level2_offset, level2_source, trans_two, spread)
        inc = lax.all_to_all(
            inc.reshape(count, grand, columns, chunk), "box", split_axis=0, concat_axis=0, tiled=True
        )
        inc = inc.swapaxes(0, 1)
    else:
        inc = weighted_lists(spread, trans_two, level2_offset, level2_source).astype(BF16)
        inc = lax.all_to_all(
            inc.reshape(count, grand, chunk, columns), "box", split_axis=0, concat_axis=0, tiled=True
        )
        inc = inc.swapaxes(0, 1)
        inc = inc.reshape(grand, samples2 // 128, 128, columns).swapaxes(2, 3)

    pieces, evens = [], []
    for one in range(splits):
        pieces.append(lax.ppermute(swapped[one], "box", up))
    for one in range(splits):
        evens.append(lax.ppermute(swapped[one], "box", pair_down))
    high_odd = lax.ppermute(high, ("box", "shift"), odd_swap)

    wide = (parents, children * unknowns, columns)
    around, unfold = rise(folded, turned, high.reshape(wide))
    across = level1(
        place, level1_offset, level1_source, trans_one, folded, low.reshape(wide), around
    )
    low, across = lax.optimization_barrier((low, across))
    near_parts, arrived = [None] * splits, [None] * splits
    for one in reversed(range(splits)):
        mine, theirs = near(
            place, near_index.T, near_blocks, low, field, high, high_odd,
            swapped, pieces[one:], evens[: one + 1], one * part, part,
        )
        near_parts[one] = mine
        arrived[one] = lax.ppermute(theirs, "shift", swap)

    total = downward(
        place, sigma, inc, interp_two, across, unfold, field, near_parts, arrived[-1], shifts
    )
    total = join(place, total, arrived[0])
    return total[None]


def solution(mesh):
    in_specs = (
        P("shift", "box", None, None),
        P("shift", None),
        P("box", None, "shift", None),
        P("box", None),
        P(),
        P(),
        P(),
        P(),
        P("box", None),
        P("box", None),
        P(None, "box"),
        P(),
        P(),
    )
    out_specs = P("shift", "box", None, None)

    return jax.shard_map(body, mesh=mesh, in_specs=in_specs, out_specs=out_specs, check_vma=False)
```

```python
import functools

import jax
import jax.numpy as jnp
from jax import lax
from jax.experimental import pallas as pl
from jax.experimental.pallas import tpu as pltpu
from jax.sharding import PartitionSpec as P


F32 = jnp.float32
BF16 = jnp.bfloat16
NT = (((1,), (1,)), ((), ()))


def vmem():
    return pl.BlockSpec(memory_space=pltpu.VMEM)


def smem():
    return pl.BlockSpec(memory_space=pltpu.SMEM)


def cost(flops, moved):
    return pl.CostEstimate(flops=flops, bytes_accessed=moved, transcendentals=0)


def params(mib):
    return pltpu.CompilerParams(vmem_limit_bytes=mib << 20)


def fold_kernel(one_ref, radiate_ref, field_ref, fold_ref, upper_ref, turned_ref):
    children, _, _ = one_ref.shape
    unknowns = radiate_ref.shape[1]
    pair, _, columns = field_ref.shape

    @pl.when(pl.program_id(0) == 0)
    def _():
        for child in range(children):
            fold_ref[:, child * unknowns : (child + 1) * unknowns] = jnp.dot(
                one_ref[child], radiate_ref[...], preferred_element_type=F32
            ).astype(BF16)

    wide = jnp.concatenate([field_ref[one] for one in range(pair)], axis=1)
    pattern = jnp.dot(fold_ref[...], wide, preferred_element_type=F32)
    for one in range(pair):
        mine = pattern[:, one * columns : (one + 1) * columns]
        upper_ref[one] = mine.astype(BF16)
        turned_ref[one] = mine.T.astype(BF16)


def fold(interp_one, radiate, field):
    children, samples1, _ = interp_one.shape
    unknowns = radiate.shape[1]
    parents, width, columns = field.shape
    pair = 2 if parents % 2 == 0 else 1
    return pl.pallas_call(
        fold_kernel,
        grid=(parents // pair,),
        out_shape=(
            jax.ShapeDtypeStruct((samples1, children * unknowns), BF16),
            jax.ShapeDtypeStruct((parents, samples1, columns), BF16),
            jax.ShapeDtypeStruct((parents, columns, samples1), BF16),
        ),
        in_specs=[
            pl.BlockSpec(interp_one.shape, lambda i: (0, 0, 0)),
            pl.BlockSpec(radiate.shape, lambda i: (0, 0)),
            pl.BlockSpec((pair, width, columns), lambda i: (i, 0, 0)),
        ],
        out_specs=(
            pl.BlockSpec((samples1, children * unknowns), lambda i: (0, 0)),
            pl.BlockSpec((pair, samples1, columns), lambda i: (i, 0, 0)),
            pl.BlockSpec((pair, columns, samples1), lambda i: (i, 0, 0)),
        ),
        compiler_params=params(56),
        cost_estimate=cost(3 * 10**9, 6 * 2**20),
        name="fold",
    )(interp_one, radiate, field)


def coarse_kernel(two_ref, upper_ref, out_ref):
    total = jnp.dot(two_ref[0], upper_ref[0], preferred_element_type=F32)
    for child in range(1, two_ref.shape[0]):
        total += jnp.dot(two_ref[child], upper_ref[child], preferred_element_type=F32)
    out_ref[0] = total.astype(BF16)


def coarsen(interp_two, upper):
    children, samples2, samples1 = interp_two.shape
    parents, _, columns = upper.shape
    grand = parents // children
    rows = min(samples2, 256)
    return pl.pallas_call(
        coarse_kernel,
        grid=(samples2 // rows, grand),
        out_shape=jax.ShapeDtypeStruct((grand, samples2, columns), BF16),
        in_specs=[
            pl.BlockSpec((children, rows, samples1), lambda q, g: (0, q, 0)),
            pl.BlockSpec((children, samples1, columns), lambda q, g: (g, 0, 0)),
        ],
        out_specs=pl.BlockSpec((1, rows, columns), lambda q, g: (g, q, 0)),
        compiler_params=params(56),
        cost_estimate=cost(4 * 10**9, 18 * 2**20),
        name="coarsen",
    )(interp_two, upper)


def live_count(source_ref, row):
    total = jnp.int32(0)
    for slot in range(source_ref.shape[1]):
        total += (source_ref[row, slot] >= 0).astype(jnp.int32)
    return total


def list_sum(offset_ref, source_ref, box, count, shape, weight_at, pattern_at, base):
    unroll = next(n for n in (4, 2, 1) if source_ref.shape[1] % n == 0)

    def add(trip, total):
        for one in range(unroll):
            slot = trip * unroll + one
            named = source_ref[box, slot]
            live = named >= 0
            weight = weight_at(offset_ref[box, slot]) * live.astype(F32)
            total = total + weight * pattern_at(jnp.where(live, named - base, 0))
        return total

    trips = (count + unroll - 1) // unroll
    return lax.fori_loop(0, trips, add, jnp.zeros(shape, F32))


def level2_kernel(offset_ref, source_ref, table_ref, pattern_ref, out_ref, turned_ref):
    boxes = pattern_ref.shape[0]

    def turn(box, carry):
        turned_ref[box] = pattern_ref[box].astype(F32).T
        return carry

    lax.fori_loop(0, boxes, turn, 0)

    def per_box(box, carry):
        total = list_sum(
            offset_ref, source_ref, box, live_count(source_ref, box), turned_ref.shape[1:],
            lambda offset: table_ref[pl.ds(offset, 1), :], lambda source: turned_ref[source], 0,
        )
        out_ref[box] = total.astype(BF16)
        return carry

    lax.fori_loop(0, out_ref.shape[0], per_box, 0)


def level2(offset, source, table, pattern):
    boxes, samples, columns = pattern.shape
    return pl.pallas_call(
        level2_kernel,
        out_shape=jax.ShapeDtypeStruct((offset.shape[0], columns, samples), BF16),
        in_specs=[smem(), smem(), vmem(), vmem()],
        out_specs=vmem(),
        scratch_shapes=[pltpu.VMEM((boxes, columns, samples), F32)],
        compiler_params=params(8),
        cost_estimate=cost(3 * 10**9, 2 * 2**20),
        name="level2",
    )(offset, source, table, pattern)


def weighted_lists(pattern, table, offsets, sources):
    live = sources >= 0
    weights = table[offsets] * live[:, :, None].astype(F32)
    picked = pattern[jnp.where(live, sources, 0)]
    return jnp.einsum("cjk,cjkr->ckr", weights, picked, preferred_element_type=F32)


def part_index(which, per):
    return lambda i: (jnp.clip(i - which * per, 0, per - 1), 0, 0)


def rise_kernel(fold_ref, turned_ref, high_ref, around_ref, unfold_ref):
    pair, _, columns = high_ref.shape

    @pl.when(pl.program_id(0) == 0)
    def _():
        for first in range(0, fold_ref.shape[1], 128):
            unfold_ref[first : first + 128, :] = fold_ref[:, first : first + 128].T

    wide = jnp.concatenate([high_ref[one] for one in range(pair)], axis=1)
    pattern = jnp.dot(fold_ref[...], wide, preferred_element_type=F32)
    for one in range(pair):
        around_ref[0, one] = turned_ref[one].astype(F32)
        around_ref[1, one] = pattern[:, one * columns : (one + 1) * columns].T.astype(BF16).astype(F32)


def rise(folded, turned, high):
    parents, columns, samples1 = turned.shape
    width = high.shape[1]
    pair = 2 if parents % 2 == 0 else 1
    return pl.pallas_call(
        rise_kernel,
        grid=(parents // pair,),
        out_shape=(
            jax.ShapeDtypeStruct((2, parents, columns, samples1), F32),
            jax.ShapeDtypeStruct((folded.shape[1], folded.shape[0]), BF16),
        ),
        in_specs=[
            pl.BlockSpec(folded.shape, lambda i: (0, 0)),
            pl.BlockSpec((pair, columns, samples1), lambda i: (i, 0, 0)),
            pl.BlockSpec((pair, width, columns), lambda i: (i, 0, 0)),
        ],
        out_specs=(
            pl.BlockSpec((2, pair, columns, samples1), lambda i: (0, i, 0, 0)),
            pl.BlockSpec((folded.shape[1], folded.shape[0]), lambda i: (0, 0)),
        ),
        compiler_params=params(56),
        cost_estimate=cost(2 * 10**9, 10 * 2**20),
        name="rise",
    )(folded, turned, high)


def level1_kernel(
    place_ref, offset_ref, source_ref, table_ref, fold_ref, around_ref, *rest,
):
    low_refs, (across_ref, rim_ref, rows_ref, sem) = rest[:-4], rest[-4:]
    step = pl.program_id(0)
    each = pl.num_programs(0) // len(low_refs)
    pair, _, columns = low_refs[0].shape
    parents, _, samples1 = across_ref.shape
    width = rows_ref.shape[2]

    def around(which):
        return pltpu.make_async_copy(
            around_ref.at[which], rim_ref.at[pl.ds((which + 1) * parents, parents)], sem.at[which]
        )

    @pl.when(step == 0)
    def _():
        around(0).start()
        around(1).start()
        for part in range(rows_ref.shape[0]):
            rows_ref[part] = table_ref[:, part * width : (part + 1) * width]

    def lows(which):
        return jnp.concatenate([low_refs[which][one] for one in range(pair)], axis=1)

    wide = lows(0)
    for which in range(1, len(low_refs)):
        wide = jnp.where(step // each == which, lows(which), wide)
    pattern = jnp.dot(fold_ref[...], wide, preferred_element_type=F32)
    for one in range(pair):
        rim_ref[step * pair + one] = (
            pattern[:, one * columns : (one + 1) * columns].T.astype(BF16).astype(F32)
        )

    @pl.when(step == pl.num_programs(0) - 1)
    def _():
        around(0).wait()
        around(1).wait()

        def per_box(box, carry):
            count = live_count(source_ref, box)
            for part in range(samples1 // width):
                lanes = slice(part * width, (part + 1) * width)
                across_ref[box, :, lanes] = list_sum(
                    offset_ref, source_ref, box, count, (columns, width),
                    lambda offset: rows_ref[part, pl.ds(offset, 1), :],
                    lambda source: rim_ref[source, :, lanes],
                    place_ref[0] * parents - parents,
                )
            return carry

        lax.fori_loop(0, parents, per_box, 0)


def level1(place, offset, source, table, folded, lows, around):
    _, parents, columns, samples1 = around.shape
    held, width, _ = lows[0].shape
    pair = 2 if held % 2 == 0 else 1
    return pl.pallas_call(
        level1_kernel,
        grid=(parents // pair,),
        out_shape=jax.ShapeDtypeStruct((parents, columns, samples1), F32),
        in_specs=[smem()] * 3
        + [
            pl.BlockSpec(table.shape, lambda i: (0, 0)),
            pl.BlockSpec(folded.shape, lambda i: (0, 0)),
            pl.BlockSpec(memory_space=pl.ANY),
        ]
        + [
            pl.BlockSpec((pair, width, columns), part_index(which, held // pair))
            for which in range(len(lows))
        ],
        out_specs=pl.BlockSpec((parents, columns, samples1), lambda i: (0, 0, 0)),
        scratch_shapes=[
            pltpu.VMEM((3 * parents, columns, samples1), F32),
            pltpu.VMEM((samples1 // 128, table.shape[0], 128), F32),
            pltpu.SemaphoreType.DMA((2,)),
        ],
        compiler_params=params(56),
        cost_estimate=cost(6 * 10**9, 12 * 2**20),
        name="level1",
    )(place, offset, source, table, folded, around, *lows)


def near_kernel(
    place_ref, index_ref, blocks_ref, own_ref, high_ref, odd_ref, *rest, first, count, cuts,
):
    low_refs, swapped_refs = rest[: cuts[0]], rest[cuts[0] : cuts[1]]
    piece_refs, even_refs = rest[cuts[1] : cuts[2]], rest[cuts[2] : -4]
    mine_ref, theirs_ref, field_ref, sem = rest[-4:]
    step = pl.program_id(0)
    place = place_ref[0]
    boxes, _, columns = own_ref.shape
    chunk, slots = blocks_ref.shape[:2]

    def into(ref, source, length, target, side, lane):
        return pltpu.make_async_copy(
            ref.at[pl.ds(source, length)],
            field_ref.at[pl.ds(target, length), :, pl.ds(side * columns, columns)],
            sem.at[lane],
        )

    copies = [
        into(own_ref, 0, boxes, boxes, 0, 0),
        into(high_ref, 0, first + count, 2 * boxes, 0, 1),
    ]
    lane = 2
    for refs, target, side in ((low_refs, first, 0), (swapped_refs, boxes, 1), (piece_refs, first, 1)):
        for one, ref in enumerate(refs):
            length = ref.shape[0]
            copies.append(into(ref, 0, length, target + one * length, side, lane))
            lane += 1
    even = []
    for one, ref in enumerate(even_refs):
        length = ref.shape[0]
        even.append(into(ref, 0, length, 2 * boxes + one * length, 1, lane))
        lane += 1
    odd = into(odd_ref, 0, first + count, 2 * boxes, 1, lane)

    @pl.when(step == 0)
    def _():
        for copy in copies:
            copy.start()

        @pl.when(place % 2 == 0)
        def _():
            for copy in even:
                copy.start()
            for copy in even:
                copy.wait()

        @pl.when(place % 2 == 1)
        def _():
            odd.start()
            odd.wait()

        for copy in copies:
            copy.wait()

    base = place * boxes - boxes
    for box in range(chunk):
        row = first + step * chunk + box
        total = None
        for slot in range(0, slots, 2):
            left, right = [], []
            for one in range(slot, min(slot + 2, slots)):
                block = blocks_ref[box, one]
                if one == 0:
                    where = boxes + row
                else:
                    named = index_ref[one, row]
                    live = named >= 0
                    where = jnp.where(live, named - base, boxes)
                    block = jnp.where(live, block, jnp.zeros_like(block))
                left.append(block)
                right.append(field_ref[where])
            part = jnp.dot(
                jnp.concatenate(left, axis=1),
                jnp.concatenate(right, axis=0),
                preferred_element_type=F32,
            )
            total = part if total is None else total + part
        mine_ref[box] = total[:, :columns]
        theirs_ref[box] = total[:, columns:].astype(BF16)


def near(place, index, blocks, own, high, odd, lows, swapped, pieces, evens, first, count):
    boxes, unknowns, columns = own.shape
    _, slots, rows, _ = blocks.shape
    chunk = min(8, count)
    lanes = len(lows) + len(swapped) + len(pieces) + len(evens)
    hbm = pl.BlockSpec(memory_space=pl.ANY)
    return pl.pallas_call(
        functools.partial(
            near_kernel, first=first, count=count,
            cuts=(len(lows), len(lows + swapped), len(lows + swapped + pieces)),
        ),
        grid=(count // chunk,),
        out_shape=(
            jax.ShapeDtypeStruct((count, rows, columns), F32),
            jax.ShapeDtypeStruct((count, rows, columns), BF16),
        ),
        in_specs=[
            smem(),
            smem(),
            pl.BlockSpec((chunk, slots, rows, unknowns), lambda i: (first // chunk + i, 0, 0, 0)),
        ]
        + [hbm] * (3 + lanes),
        out_specs=(pl.BlockSpec((chunk, rows, columns), lambda i: (i, 0, 0)),) * 2,
        scratch_shapes=[
            pltpu.VMEM((3 * boxes, unknowns, 2 * columns), BF16),
            pltpu.SemaphoreType.DMA((3 + lanes,)),
        ],
        compiler_params=params(56),
        cost_estimate=cost(count * 2 * 10**8, 14 * 2**20 + count * 10**5),
    )(place, index, blocks, own, high, odd, *lows, *swapped, *pieces, *evens)


def down_kernel(place_ref, sigma_ref, inc_ref, two_ref, across_ref, unfold_ref, field_ref, *rest, children, pair, parts, shifts):
    near_refs, early_ref, (out_ref, flat_ref, local_ref) = rest[:parts], rest[parts], rest[parts + 1 :]
    chunks, columns, lanes = inc_ref.shape[1:]
    step = pl.program_id(0)
    span_of = pl.num_programs(0) // parts

    @pl.when(step % children == 0)
    def _():
        for one in range(chunks):
            flat_ref[:, one * lanes : (one + 1) * lanes] = inc_ref[0, one]

    down = jnp.dot(flat_ref[...], two_ref[0], preferred_element_type=F32)
    local_ref[pl.ds((step % pair) * columns, columns), :] = (down + across_ref[0]).astype(BF16)

    @pl.when(step % pair == pair - 1)
    def _():
        far = lax.dot_general(unfold_ref[...], local_ref[...], NT, preferred_element_type=F32)
        boxes, unknowns, _ = out_ref.shape
        per = boxes // pair
        half = unknowns // 2
        re, im = sigma_ref[0, 0], sigma_ref[0, 1]
        for one in range(pair):
            mine = far[:, one * columns : (one + 1) * columns].reshape(per, unknowns, columns)
            span = slice(one * per, (one + 1) * per)
            real = field_ref[span, :half, :].astype(F32)
            imag = field_ref[span, half:, :].astype(F32)
            out_ref[span, :half, :] = mine[:, :half] - (re * real - im * imag)
            out_ref[span, half:, :] = mine[:, half:] - (re * imag + im * real)
        rows = near_refs[0].shape[1]
        for shift in range(shifts):
            for part, near_ref in enumerate(near_refs):

                @pl.when((place_ref[1] == shift) & (step // span_of == part))
                def _():
                    out_ref[:, shift * rows : (shift + 1) * rows, :] += near_ref[...]

            @pl.when((place_ref[1] == shift) & (step // span_of == parts - 1))
            def _():
                there = shifts - 1 - shift
                out_ref[:, there * rows : (there + 1) * rows, :] += early_ref[...].astype(F32)


def downward(place, sigma, inc, interp_two, across, unfold, field, near_parts, early, shifts):
    grand, chunks, columns, lanes = inc.shape
    children, samples2, samples1 = interp_two.shape
    boxes, unknowns, _ = field.shape
    rows = near_parts[0].shape[1]
    parts = len(near_parts)
    pair = 2 if children % 2 == 0 else 1
    per = pair * (boxes // across.shape[0])
    each = boxes // per // parts
    return pl.pallas_call(
        functools.partial(down_kernel, children=children, pair=pair, parts=parts, shifts=shifts),
        grid=(grand * children,),
        out_shape=jax.ShapeDtypeStruct((boxes, unknowns, columns), F32),
        in_specs=[
            smem(),
            smem(),
            pl.BlockSpec((1, chunks, columns, lanes), lambda c: (c // children, 0, 0, 0)),
            pl.BlockSpec((1, samples2, samples1), lambda c: (c % children, 0, 0)),
            pl.BlockSpec((1, columns, samples1), lambda c: (c, 0, 0)),
            pl.BlockSpec(unfold.shape, lambda c: (0, 0)),
            pl.BlockSpec((per, unknowns, columns), lambda c: (c // pair, 0, 0)),
        ]
        + [
            pl.BlockSpec((per, rows, columns), lambda c, part=part: part_index(part, each)(c // pair))
            for part in list(range(parts)) + [parts - 1]
        ],
        out_specs=pl.BlockSpec((per, unknowns, columns), lambda c: (c // pair, 0, 0)),
        scratch_shapes=[
            pltpu.VMEM((columns, chunks * lanes), BF16),
            pltpu.VMEM((pair * columns, samples1), BF16),
        ],
        compiler_params=params(54),
        cost_estimate=cost(6 * 10**9, 30 * 2**20),
        name="downward",
    )(place, sigma, inc, interp_two, across, unfold, field, *near_parts, early)


def join_kernel(place_ref, total_ref, part_ref, out_ref):
    out_ref[...] = total_ref[...] + part_ref[...].astype(F32)


def join(place, total, part):
    count, rows, columns = part.shape
    step = min(8, count)
    half = pl.BlockSpec((step, rows, columns), lambda i, place_ref: (i, 1 - place_ref[1], 0))
    return pl.pallas_call(
        join_kernel,
        grid_spec=pltpu.PrefetchScalarGridSpec(
            num_scalar_prefetch=1,
            grid=(count // step,),
            in_specs=[half, pl.BlockSpec((step, rows, columns), lambda i, place_ref: (i, 0, 0))],
            out_specs=half,
        ),
        out_shape=jax.ShapeDtypeStruct(total.shape, F32),
        input_output_aliases={1: 0},
        compiler_params=params(10),
        cost_estimate=cost(10**7, 3 * 2**20),
        name="join",
    )(place, total, part)


def body(
    vectors, sigma, near_blocks, near_index, radiate, interp_one, interp_two, trans_one,
    level1_source, level1_offset, trans_two, level2_source, level2_offset,
):
    field = vectors[0]
    boxes, unknowns, columns = field.shape
    children, _, _ = interp_one.shape
    samples2 = interp_two.shape[1]
    parents = boxes // children
    grand = parents // children
    count = lax.axis_size("box")
    shifts = lax.axis_size("shift")
    place = jnp.stack([lax.axis_index("box"), lax.axis_index("shift")]).astype(jnp.int32)

    up = [(i, i + 1) for i in range(count - 1)]
    down = [(i + 1, i) for i in range(count - 1)]
    swap = [(s, shifts - 1 - s) for s in range(shifts)]
    pair_down = [(i + 1, i) for i in range(0, count - 1, 2)]
    odd_swap = [
        (i * shifts + s, i * shifts + shifts - 1 - s) for i in range(1, count, 2) for s in range(shifts)
    ]

    splits = 2
    part = boxes // splits
    swapped, lows = [None] * splits, [None] * splits
    for one in reversed(range(splits)):
        mine = lax.slice_in_dim(field, one * part, (one + 1) * part, axis=0)
        swapped[one] = lax.ppermute(mine, "shift", swap)
        lows[one] = lax.ppermute(mine, "box", up)
    high = lax.ppermute(field, "box", down)

    folded, upper, turned = fold(
        interp_one, radiate, field.reshape(parents, children * unknowns, columns)
    )
    coarse = coarsen(interp_two, upper)
    chunk = samples2 // count
    pieces = coarse.reshape(grand, count, chunk, columns).swapaxes(0, 1)
    spread = lax.all_to_all(pieces, "box", split_axis=0, concat_axis=0, tiled=True)
    spread = spread.reshape(count * grand, chunk, columns)
    if chunk % 128 == 0:
        inc = level2(level2_offset, level2_source, trans_two, spread)
        inc = lax.all_to_all(
            inc.reshape(count, grand, columns, chunk), "box", split_axis=0, concat_axis=0, tiled=True
        )
        inc = inc.swapaxes(0, 1)
    else:
        inc = weighted_lists(spread, trans_two, level2_offset, level2_source).astype(BF16)
        inc = lax.all_to_all(
            inc.reshape(count, grand, chunk, columns), "box", split_axis=0, concat_axis=0, tiled=True
        )
        inc = inc.swapaxes(0, 1)
        inc = inc.reshape(grand, samples2 // 128, 128, columns).swapaxes(2, 3)

    pieces, evens = [], []
    for one in range(splits):
        pieces.append(lax.ppermute(swapped[one], "box", up))
    for one in range(splits):
        evens.append(lax.ppermute(swapped[one], "box", pair_down))
    high_odd = lax.ppermute(high, ("box", "shift"), odd_swap)

    wide = (parents, children * unknowns, columns)
    around, unfold = rise(folded, turned, high.reshape(wide))
    halves = [low.reshape((parents // splits,) + wide[1:]) for low in lows]
    across = level1(place, level1_offset, level1_source, trans_one, folded, halves, around)
    high, across = lax.optimization_barrier((high, across))
    near_parts, arrived = [None] * splits, [None] * splits
    for one in reversed(range(splits)):
        mine, theirs = near(
            place, near_index.T, near_blocks, field, high, high_odd,
            lows[one:], swapped, pieces[one:], evens[: one + 1], one * part, part,
        )
        near_parts[one] = mine
        arrived[one] = lax.ppermute(theirs, "shift", swap)

    total = downward(
        place, sigma, inc, interp_two, across, unfold, field, near_parts, arrived[-1], shifts
    )
    total = join(place, total, arrived[0])
    return total[None]


def solution(mesh):
    in_specs = (
        P("shift", "box", None, None),
        P("shift", None),
        P("box", None, "shift", None),
        P("box", None),
        P(),
        P(),
        P(),
        P(),
        P("box", None),
        P("box", None),
        P(None, "box"),
        P(),
        P(),
    )
    out_specs = P("shift", "box", None, None)

    return jax.shard_map(body, mesh=mesh, in_specs=in_specs, out_specs=out_specs, check_vma=False)
```
